32 devices in a mesh: chan: 4 (over z), tm: 2 (over y), row: 4 (over x, core).
Axes of the slice: x: 2, y: 2, z: 4, core: 2. Of those that a mesh axis runs over, the one named last changes fastest.
Arguments:
- samples: bfloat16 [8, 4096, 4096], P(('tm', 'row'), None, 'chan'), may hold values from -6 to 6
- channel_index: int32 [16], replicated, may hold values from 1 to 2047
- gain_real: float32 [16, 4096], P(None, 'chan'), may hold values from -4 to 4
- gain_imag: float32 [16, 4096], P(None, 'chan'), may hold values from -4 to 4
- flags: int32 [2048], P('chan'), may hold values 0 or 1
Outputs:
- visibility: bfloat16 [2, 16, 4096, 4096], P(None, 'chan', 'row', 'tm')
The draws below stay inside these ranges and needn't reach their ends.
Inputs may be any that keep to these rules, and one draw needn't show every extreme that they name: `channel_index`: channel numbers, not necessarily distinct.
All inputs are finite; a program needn't handle non-finite values. No bound on the sum of `flags` on one device may be relied on, other than what follows from the above.
Results may differ from the reference program's by a relative error of at most 0.0056.
Values may be sent and summed in bfloat16 or wider, within the bound.
No kernel may reach another device: no remote copies, remote signals or barrier semaphores. Data moves between devices by JAX's collectives and lax.ppermute only.
A program may use at most 256 MiB of HBM per device.

```python
import math
import jax
import jax.numpy as jnp
from jax import lax

P_SIZE = 4096
TAPS = 4
INPUTS = 4096
CHANNELS = 16
ANTENNAS = 2048
FRAMES = 8


def place_ends(values, rng, low, high):
    index_at = [jax.random.randint(jax.random.fold_in(rng, axis), (), 0, length) for axis, length in enumerate(values.shape)]
    longest = values.shape.index(max(values.shape))
    beside = index_at[:longest] + [(index_at[longest] + 1) % values.shape[longest]] + index_at[longest + 1:]
    return values.at[tuple(index_at)].set(low).at[tuple(beside)].set(high)


def block_levels(own_key, shape, cuts, smallest, largest):
    def one(axis_at, shards_of):
        draws = jax.random.uniform(jax.random.fold_in(jax.random.fold_in(own_key, 6), axis_at), (shards_of,), jnp.float32, smallest / len(cuts), largest / len(cuts))
        return jnp.repeat(jnp.exp(draws), shape[axis_at] // shards_of).reshape((-1,) + (1,) * (len(shape) - axis_at - 1))

    level = one(*cuts[0])
    for cut in cuts[1:]:
        level = level * one(*cut)
    return level


def normal_values(own_key, shape, scale, most, pieces=(), kind=jnp.bfloat16):
    values = jax.random.normal(own_key, shape, jnp.float32) * scale
    if len(pieces) > 0:
        values = block_levels(own_key, shape, pieces, -0.22, 0.18) * values
    return jnp.clip(values, min=-most, max=most).astype(kind)


def setup_inputs(seed: int = 0) -> dict:
    key_of = jax.random.split(jax.random.key(seed), 6)
    return {
        "samples": normal_values(key_of[0], (FRAMES, P_SIZE, INPUTS), 1.0, 6.0, ((0, 8), (2, 4))),
        "channel_index": place_ends(jax.random.randint(key_of[1], (CHANNELS,), 1, P_SIZE // 2), jax.random.fold_in(key_of[1], 1), 1, (P_SIZE // 2) - 1).astype(jnp.int32),
        "gain_real": normal_values(key_of[2], (CHANNELS, INPUTS), 0.7, 4.0, ((1, 4),), jnp.float32),
        "gain_imag": normal_values(key_of[3], (CHANNELS, INPUTS), 0.7, 4.0, ((1, 4),), jnp.float32),
        "flags": place_ends((jax.random.randint(key_of[4], (ANTENNAS,), 0, 8) < 7).astype(jnp.int32), jax.random.fold_in(key_of[4], 1), 0, 1),
    }


def filter_taps():
    sample_index = jnp.arange(TAPS * P_SIZE, dtype=jnp.int32).astype(jnp.float32)
    centered = (sample_index + 0.5 - TAPS * P_SIZE / 2) / P_SIZE
    hann_taper = 0.5 - 0.5 * jnp.cos(2.0 * math.pi * (sample_index + 0.5) / (TAPS * P_SIZE))
    return (jnp.sinc(centered) * hann_taper).reshape(TAPS, P_SIZE)

def dft_table(channel_index):
    points = jnp.arange(P_SIZE, dtype=jnp.int32)
    phase_index = channel_index[:, None] * points[None, :] % P_SIZE
    angles = 2.0 * math.pi * phase_index.astype(jnp.float32) / P_SIZE
    scale = 1.0 / math.sqrt(P_SIZE)
    return jnp.concatenate([jnp.cos(angles) * scale, -jnp.sin(angles) * scale], 0)

def reference(samples, channel_index, gain_real, gain_imag, flags):
    filters = filter_taps()
    table = dft_table(channel_index)
    padded = jnp.concatenate([jnp.zeros((TAPS - 1, P_SIZE, INPUTS), jnp.bfloat16), samples], 0)

    def one_frame(frame):
        window = lax.dynamic_slice_in_dim(padded, frame, TAPS, 0).astype(jnp.float32)
        weighted = lax.optimization_barrier(jnp.sum(filters[:, :, None] * window, 0))
        return jnp.dot(table, weighted, precision=lax.Precision.HIGHEST)
    spectra = lax.map(one_frame, jnp.arange(FRAMES, dtype=jnp.int32))
    spec_re = spectra[:, :CHANNELS]
    spec_im = spectra[:, CHANNELS:]
    usable = jnp.repeat(flags, 2).astype(jnp.float32)
    volt_re = (usable * (gain_real * spec_re - gain_imag * spec_im)).astype(jnp.bfloat16)
    volt_im = (usable * (gain_real * spec_im + gain_imag * spec_re)).astype(jnp.bfloat16)

    def one_channel(pair):
        real_part, imag_part = pair
        left_side = jnp.concatenate([real_part, imag_part], 0)
        right_side = jnp.concatenate([jnp.concatenate([real_part, -imag_part], 1), jnp.concatenate([imag_part, real_part], 1)], 0)
        product = lax.dot_general(left_side, right_side, (((0,), (0,)), ((), ())), preferred_element_type=jnp.float32)
        result = jnp.stack([product[:, :INPUTS], product[:, INPUTS:]], 0) / FRAMES
        return result.astype(jnp.bfloat16)
    per_channel = lax.map(one_channel, (volt_re.transpose(1, 0, 2), volt_im.transpose(1, 0, 2)))
    return per_channel.transpose(1, 0, 2, 3)
```

```python
import functools
import math

import jax
import jax.numpy as jnp
from jax import lax
from jax.experimental import pallas as pl
from jax.experimental.pallas import tpu as pltpu
from jax.sharding import PartitionSpec as P

TAPS = 4
LANES = 128
PAIR_TAPS = (1, 2)
SPLITS = 8
TILE = 512
VMEM_BYTES = 48 << 20
FRAME_AXES = ("tm", "row")

IN_VMEM = pl.BlockSpec(memory_space=pltpu.VMEM)
IN_HBM = pl.BlockSpec(memory_space=pltpu.HBM)


def in_hbm(*arrays):
    return [pltpu.with_memory_space_constraint(a, pltpu.HBM) for a in arrays]


def shifted(value, axis, by, wrap):
    peers = lax.axis_size(axis)
    pairs = [(i, (i + by) % peers) for i in range(peers) if wrap or i + by < peers]
    return lax.ppermute(value, axis, pairs)


def sine_quarter(x):
    y = x * x
    acc = 1.0 / 6227020800.0
    for k in (-1.0 / 39916800.0, 1.0 / 362880.0, -1.0 / 5040.0, 1.0 / 120.0, -1.0 / 6.0, 1.0):
        acc = acc * y + k
    return acc * x


def turn(m, quarter):
    q = (m + quarter // 2) >> (quarter.bit_length() - 1)
    r = (m - q * quarter).astype(jnp.float32) * (math.pi / 2 / quarter)
    y = r * r
    cos = ((((-1.0 / 3628800.0 * y + 1.0 / 40320.0) * y - 1.0 / 720.0) * y + 1.0 / 24.0) * y - 0.5) * y + 1.0
    sin = ((((1.0 / 362880.0 * y - 1.0 / 5040.0) * y + 1.0 / 120.0) * y - 1.0 / 6.0) * y + 1.0) * r
    odd = (q & 1) == 1
    first = jnp.where(odd, sin, cos)
    second = jnp.where(odd, cos, sin)
    return jnp.where(((q + 1) & 2) != 0, -first, first), jnp.where((q & 2) != 0, -second, second)


def front_body(
    index_hbm, samples_ref, gr_hbm, gi_hbm, flags_hbm,
    own_ref, one_ref, two_ref, three_ref,
    index_ref, gr_ref, gi_ref, flags_ref, block_ref, filter_ref, table_ref, acc_ref, sems, small_sems,
    *, groups,
):
    points, width = block_ref.shape
    channels = gr_ref.shape[0]
    cg = channels // groups
    rows = 2 * channels
    quarter = points // 4
    index_copy = pltpu.make_async_copy(index_hbm, index_ref, small_sems.at[0])
    index_copy.start()
    part = points // SPLITS
    fetches = [
        pltpu.make_async_copy(
            samples_ref.at[0, pl.ds(i * part, part), :], block_ref.at[pl.ds(i * part, part), :], sems.at[i]
        )
        for i in range(SPLITS)
    ]
    for copy in fetches:
        copy.start()
    others = [
        pltpu.make_async_copy(src, dst, small_sems.at[1 + i])
        for i, (src, dst) in enumerate(((gr_hbm, gr_ref), (gi_hbm, gi_ref), (flags_hbm, flags_ref)))
    ]
    for copy in others:
        copy.start()

    spans = points // LANES
    at = lax.broadcasted_iota(jnp.int32, (spans, LANES), 0) * LANES
    at = at + lax.broadcasted_iota(jnp.int32, (spans, LANES), 1)
    u = (at.astype(jnp.float32) + 0.5) * (1.0 / points)
    sn = sine_quarter(u * (math.pi / 2))
    cs = sine_quarter((1.0 - u) * (math.pi / 2))
    sp = 2.0 * sn * cs * (1.0 / math.pi / math.sqrt(points))
    filter_ref[0] = sp / (u - 2.0) * (0.5 - 0.5 * cs)
    filter_ref[1] = -sp / (u - 1.0) * (0.5 + 0.5 * sn)
    filter_ref[2] = sp / u * (0.5 + 0.5 * cs)
    filter_ref[3] = -sp / (u + 1.0) * (0.5 - 0.5 * sn)

    rho = lax.broadcasted_iota(jnp.int32, (rows, LANES), 0)
    lane = lax.broadcasted_iota(jnp.int32, (rows, LANES), 1)
    chan = lax.div(rho, 2 * cg) * cg + lax.rem(rho, cg)
    imag = jnp.where(lax.rem(rho, 2 * cg) >= cg, quarter, 0)
    index_copy.wait()
    index = jnp.zeros((rows, LANES), jnp.int32)
    for c in range(channels):
        index = jnp.where(chan == c, index_ref[c], index)
    cos_a, sin_a = turn(index * lane + imag, quarter)
    cos_b, sin_b = turn(index * lane * LANES, quarter)
    for a in range(spans):
        v = cos_a * cos_b[:, a : a + 1] - sin_a * sin_b[:, a : a + 1]
        cols = slice(a * LANES, (a + 1) * LANES)
        for k in range(TAPS):
            t = filter_ref[k, a : a + 1, :] * v
            high = t.astype(jnp.bfloat16)
            table_ref[k * rows : (k + 1) * rows, cols] = high
            if k in PAIR_TAPS:
                i = TAPS + PAIR_TAPS.index(k)
                table_ref[i * rows : (i + 1) * rows, cols] = (t - high.astype(jnp.float32)).astype(jnp.bfloat16)
    for i, copy in enumerate(fetches):
        copy.wait()
        span = slice(i * part, (i + 1) * part)
        product = jnp.dot(table_ref[:, span], block_ref[span, :], preferred_element_type=jnp.float32)
        acc_ref[...] = product if i == 0 else acc_ref[...] + product

    for copy in others:
        copy.wait()
    row = lax.broadcasted_iota(jnp.int32, (LANES, 2 * LANES), 0)
    col = lax.broadcasted_iota(jnp.int32, (LANES, 2 * LANES), 1)
    spread = jnp.where(row == lax.div(col, 2), 1.0, 0.0).astype(jnp.bfloat16)
    usable = []
    for j in range(flags_ref.shape[1] // LANES):
        some = flags_ref[:, j * LANES : (j + 1) * LANES].astype(jnp.float32)
        some = jnp.broadcast_to(some, (8, LANES)).astype(jnp.bfloat16)
        usable.append(jnp.dot(some, spread, preferred_element_type=jnp.float32))
    usable = usable[0] if len(usable) == 1 else jnp.concatenate(usable, 1)
    usable = jnp.concatenate([usable] * (rows // 8), 0)
    gr, gi = [], []
    for g in range(groups):
        a, b = gr_ref[g * cg : (g + 1) * cg], gi_ref[g * cg : (g + 1) * cg]
        gr += [a, a]
        gi += [-b, b]
    gr = jnp.concatenate(gr, 0) * usable
    gi = jnp.concatenate(gi, 0) * usable
    low = lax.rem(lax.broadcasted_iota(jnp.int32, (rows, width), 0), 2 * cg) < cg
    for k, ref in ((3, own_ref), (2, one_ref), (1, two_ref), (0, three_ref)):
        s = acc_ref[k * rows : (k + 1) * rows]
        if k in PAIR_TAPS:
            i = TAPS + PAIR_TAPS.index(k)
            s = s + acc_ref[i * rows : (i + 1) * rows]
        other = jnp.where(low, pltpu.roll(s, rows - cg, 0), pltpu.roll(s, cg, 0))
        ref[...] = (gr * s + gi * other).astype(ref.dtype)


def front(samples, channel_index, gain_real, gain_imag, flags, groups):
    _, points, width = samples.shape
    channels = gain_real.shape[0]
    rows = 2 * channels
    depth = (TAPS + len(PAIR_TAPS)) * rows
    flags = flags.reshape(1, -1)
    return pl.pallas_call(
        functools.partial(front_body, groups=groups),
        name="front",
        out_shape=[jax.ShapeDtypeStruct((rows, width), jnp.float32)]
        + [jax.ShapeDtypeStruct((rows, width), jnp.bfloat16)] * 3,
        in_specs=[IN_HBM] * 5,
        out_specs=[IN_VMEM] * 4,
        scratch_shapes=[
            pltpu.SMEM(channel_index.shape, jnp.int32),
            pltpu.VMEM(gain_real.shape, jnp.float32),
            pltpu.VMEM(gain_imag.shape, jnp.float32),
            pltpu.VMEM(flags.shape, jnp.int32),
            pltpu.VMEM((points, width), samples.dtype),
            pltpu.VMEM((TAPS, points // LANES, LANES), jnp.float32),
            pltpu.VMEM((depth, points), jnp.bfloat16),
            pltpu.VMEM((depth, width), jnp.float32),
            pltpu.SemaphoreType.DMA((SPLITS,)),
            pltpu.SemaphoreType.DMA((4,)),
        ],
        compiler_params=pltpu.CompilerParams(vmem_limit_bytes=VMEM_BYTES),
    )(*in_hbm(channel_index, samples, gain_real, gain_imag, flags))


def combine_body(own_ref, one_ref, two_ref, three_ref, *refs):
    out_refs, total_ref = refs[:-1], refs[-1]
    groups, size, _ = total_ref.shape
    total = own_ref[...]
    for ref in (one_ref, two_ref, three_ref):
        total = total + ref[...].astype(jnp.float32)
    for g in range(groups):
        total_ref[g] = total[g * size : (g + 1) * size]
    me = lax.axis_index("chan")
    for j, ref in enumerate(out_refs):
        ref[...] = total_ref[lax.rem(me + j, groups)].astype(jnp.bfloat16)


def combine(own, one, two, three, groups):
    rows, width = own.shape
    piece = jax.ShapeDtypeStruct((rows // groups, width), jnp.bfloat16)
    return pl.pallas_call(
        combine_body,
        name="combine",
        out_shape=[piece] * groups,
        in_specs=[IN_VMEM] * 4,
        out_specs=[IN_VMEM] * groups,
        scratch_shapes=[pltpu.VMEM((groups, rows // groups, width), jnp.float32)],
        compiler_params=pltpu.CompilerParams(vmem_limit_bytes=VMEM_BYTES),
    )(own, one, two, three)


def correlate_body(volts_ref, out_ref, all_ref, left_ref, right_ref, tile_ref, sems, *, tile):
    frames, chunks, size, width = volts_ref.shape
    cg = size // 2
    depth = frames * size
    rows, cols = out_ref.shape[2:]
    me = lax.axis_index("chan")
    piece_of = lambda chunk: lax.rem(me - chunk + chunks, chunks)
    for f in range(frames):
        for j in range(chunks):
            all_ref[j, f * size : (f + 1) * size, :] = volts_ref[f, j].astype(jnp.float32)
    n_row, n_col = rows // width, cols // width
    lane = lax.broadcasted_iota(jnp.int32, (width, depth), 1)
    for q in range(n_row):
        turned = (all_ref[piece_of(lax.axis_index("row") * n_row + q)] * (1.0 / frames)).T
        for c in range(cg):
            mine = jnp.where(lax.rem(lane, cg) == c, turned, 0.0)
            left_ref[c, q * width : (q + 1) * width, :] = mine.astype(jnp.bfloat16)
    low = lax.rem(lax.broadcasted_iota(jnp.int32, (depth, width), 0), size) < cg
    for q in range(n_col):
        x = all_ref[piece_of(lax.axis_index("tm") * n_col + q)]
        part = slice(q * width, (q + 1) * width)
        right_ref[0, :, part] = x.astype(jnp.bfloat16)
        crossed = jnp.where(low, -pltpu.roll(x, depth - cg, 0), pltpu.roll(x, cg, 0))
        right_ref[1, :, part] = crossed.astype(jnp.bfloat16)

    high, wide = min(tile, rows), min(tile, cols)
    spots = [(top, left) for left in range(0, cols, wide) for top in range(0, rows, high)]
    total = 2 * cg

    def copy(n, s):
        top, left = spots[s]
        slot = lax.rem(n, 2)
        return pltpu.make_async_copy(
            tile_ref.at[slot, pl.ds(top, high), pl.ds(left, wide)],
            out_ref.at[lax.rem(n, 2), lax.div(n, 2), pl.ds(top, high), pl.ds(left, wide)],
            sems.at[slot, s],
        )

    def step(n, carry):
        @pl.when(n >= 2)
        def _():
            for s in range(len(spots)):
                copy(n - 2, s).wait()

        for s, (top, left) in enumerate(spots):
            product = jnp.dot(
                left_ref[lax.div(n, 2), top : top + high, :],
                right_ref[lax.rem(n, 2), :, left : left + wide],
                preferred_element_type=jnp.float32,
            )
            tile_ref[lax.rem(n, 2), top : top + high, left : left + wide] = product.astype(jnp.bfloat16)
            copy(n, s).start()
        return carry

    lax.fori_loop(0, total, step, 0)
    for n in range(total - 2, total):
        for s in range(len(spots)):
            copy(n, s).wait()


def correlate(volts, rows, cols):
    frames, chunks, size, width = volts.shape
    cg = size // 2
    depth = frames * size
    spots = (rows // min(TILE, rows)) * (cols // min(TILE, cols))
    return pl.pallas_call(
        functools.partial(correlate_body, tile=TILE),
        name="correlate",
        out_shape=jax.ShapeDtypeStruct((2, cg, rows, cols), jnp.bfloat16),
        in_specs=[IN_VMEM],
        out_specs=IN_HBM,
        scratch_shapes=[
            pltpu.VMEM((chunks, depth, width), jnp.float32),
            pltpu.VMEM((cg, rows, depth), jnp.bfloat16),
            pltpu.VMEM((2, depth, cols), jnp.bfloat16),
            pltpu.VMEM((2, rows, cols), jnp.bfloat16),
            pltpu.SemaphoreType.DMA((2, spots)),
        ],
        compiler_params=pltpu.CompilerParams(vmem_limit_bytes=VMEM_BYTES),
    )(volts)


def local(samples, channel_index, gain_real, gain_imag, flags):
    planes = lax.axis_size("chan")
    inputs_total = samples.shape[2] * planes
    own, one, two, three = front(samples, channel_index, gain_real, gain_imag, flags, planes)
    one = shifted(one, FRAME_AXES, 1, False)
    two = shifted(two, FRAME_AXES, 2, False)
    three = shifted(three, FRAME_AXES, 3, False)
    pieces = combine(own, one, two, three, planes)
    pieces = [piece if j == 0 else shifted(piece, "chan", j, True) for j, piece in enumerate(pieces)]
    volts = lax.all_gather(jnp.stack(pieces), FRAME_AXES, axis=0)
    return correlate(volts, inputs_total // lax.axis_size("row"), inputs_total // lax.axis_size("tm"))


def solution(mesh):
    in_specs = (P(("tm", "row"), None, "chan"), P(), P(None, "chan"), P(None, "chan"), P("chan"))
    out_specs = P(None, "chan", "row", "tm")
    return jax.shard_map(local, mesh=mesh, in_specs=in_specs, out_specs=out_specs, check_vma=False)
```

```python
import functools
import math

import jax
import jax.numpy as jnp
from jax import lax
from jax.experimental import pallas as pl
from jax.experimental.pallas import tpu as pltpu
from jax.sharding import PartitionSpec as P

TAPS = 4
LANES = 128
PAIR_TAPS = (1, 2)
SPLITS = 8
TILE = 512
VMEM_BYTES = 48 << 20
FRAME_AXES = ("tm", "row")

IN_VMEM = pl.BlockSpec(memory_space=pltpu.VMEM)
IN_HBM = pl.BlockSpec(memory_space=pltpu.HBM)


def in_hbm(*arrays):
    return [pltpu.with_memory_space_constraint(a, pltpu.HBM) for a in arrays]


def rotated(value, axis, by):
    peers = lax.axis_size(axis)
    return lax.ppermute(value, axis, [(i, (i + by) % peers) for i in range(peers)])


def sine_quarter(x):
    y = x * x
    acc = 1.0 / 6227020800.0
    for k in (-1.0 / 39916800.0, 1.0 / 362880.0, -1.0 / 5040.0, 1.0 / 120.0, -1.0 / 6.0, 1.0):
        acc = acc * y + k
    return acc * x


def turn(m, quarter):
    q = (m + quarter // 2) >> (quarter.bit_length() - 1)
    r = (m - q * quarter).astype(jnp.float32) * (math.pi / 2 / quarter)
    y = r * r
    cos = ((((-1.0 / 3628800.0 * y + 1.0 / 40320.0) * y - 1.0 / 720.0) * y + 1.0 / 24.0) * y - 0.5) * y + 1.0
    sin = ((((1.0 / 362880.0 * y - 1.0 / 5040.0) * y + 1.0 / 120.0) * y - 1.0 / 6.0) * y + 1.0) * r
    odd = (q & 1) == 1
    first = jnp.where(odd, sin, cos)
    second = jnp.where(odd, cos, sin)
    return jnp.where(((q + 1) & 2) != 0, -first, first), jnp.where((q & 2) != 0, -second, second)


def front_body(
    index_hbm, samples_ref, gr_hbm, gi_hbm, flags_hbm,
    keep_ref, give_ref,
    index_ref, gr_ref, gi_ref, flags_ref, block_ref, filter_ref, table_ref, acc_ref, sems, small_sems,
    *, groups,
):
    points, width = block_ref.shape
    channels = gr_ref.shape[0]
    cg = channels // groups
    rows = 2 * channels
    quarter = points // 4
    index_copy = pltpu.make_async_copy(index_hbm, index_ref, small_sems.at[0])
    index_copy.start()
    part = points // SPLITS
    fetches = [
        pltpu.make_async_copy(
            samples_ref.at[0, pl.ds(i * part, part), :], block_ref.at[pl.ds(i * part, part), :], sems.at[i]
        )
        for i in range(SPLITS)
    ]
    for copy in fetches:
        copy.start()
    others = [
        pltpu.make_async_copy(src, dst, small_sems.at[1 + i])
        for i, (src, dst) in enumerate(((gr_hbm, gr_ref), (gi_hbm, gi_ref), (flags_hbm, flags_ref)))
    ]
    for copy in others:
        copy.start()

    spans = points // LANES
    at = lax.broadcasted_iota(jnp.int32, (spans, LANES), 0) * LANES
    at = at + lax.broadcasted_iota(jnp.int32, (spans, LANES), 1)
    u = (at.astype(jnp.float32) + 0.5) * (1.0 / points)
    sn = sine_quarter(u * (math.pi / 2))
    cs = sine_quarter((1.0 - u) * (math.pi / 2))
    sp = 2.0 * sn * cs * (1.0 / math.pi / math.sqrt(points))
    filter_ref[0] = sp / (u - 2.0) * (0.5 - 0.5 * cs)
    filter_ref[1] = -sp / (u - 1.0) * (0.5 + 0.5 * sn)
    filter_ref[2] = sp / u * (0.5 + 0.5 * cs)
    filter_ref[3] = -sp / (u + 1.0) * (0.5 - 0.5 * sn)

    rho = lax.broadcasted_iota(jnp.int32, (rows, LANES), 0)
    lane = lax.broadcasted_iota(jnp.int32, (rows, LANES), 1)
    chan = lax.div(rho, 2 * cg) * cg + lax.rem(rho, cg)
    imag = jnp.where(lax.rem(rho, 2 * cg) >= cg, quarter, 0)
    index_copy.wait()
    index = jnp.zeros((rows, LANES), jnp.int32)
    for c in range(channels):
        index = jnp.where(chan == c, index_ref[c], index)
    cos_a, sin_a = turn(index * lane + imag, quarter)
    cos_b, sin_b = turn(index * lane * LANES, quarter)
    for a in range(spans):
        v = cos_a * cos_b[:, a : a + 1] - sin_a * sin_b[:, a : a + 1]
        cols = slice(a * LANES, (a + 1) * LANES)
        for k in range(TAPS):
            t = filter_ref[k, a : a + 1, :] * v
            high = t.astype(jnp.bfloat16)
            table_ref[k * rows : (k + 1) * rows, cols] = high
            if k in PAIR_TAPS:
                i = TAPS + PAIR_TAPS.index(k)
                table_ref[i * rows : (i + 1) * rows, cols] = (t - high.astype(jnp.float32)).astype(jnp.bfloat16)
    for i, copy in enumerate(fetches):
        copy.wait()
        span = slice(i * part, (i + 1) * part)
        product = jnp.dot(table_ref[:, span], block_ref[span, :], preferred_element_type=jnp.float32)
        acc_ref[...] = product if i == 0 else acc_ref[...] + product

    for copy in others:
        copy.wait()
    row = lax.broadcasted_iota(jnp.int32, (LANES, 2 * LANES), 0)
    col = lax.broadcasted_iota(jnp.int32, (LANES, 2 * LANES), 1)
    spread = jnp.where(row == lax.div(col, 2), 1.0, 0.0).astype(jnp.bfloat16)
    usable = []
    for j in range(flags_ref.shape[1] // LANES):
        some = flags_ref[:, j * LANES : (j + 1) * LANES].astype(jnp.float32)
        some = jnp.broadcast_to(some, (8, LANES)).astype(jnp.bfloat16)
        usable.append(jnp.dot(some, spread, preferred_element_type=jnp.float32))
    usable = usable[0] if len(usable) == 1 else jnp.concatenate(usable, 1)
    usable = jnp.concatenate([usable] * (rows // 8), 0)
    gr, gi = [], []
    for g in range(groups):
        a, b = gr_ref[g * cg : (g + 1) * cg], gi_ref[g * cg : (g + 1) * cg]
        gr += [a, a]
        gi += [-b, b]
    gr = jnp.concatenate(gr, 0) * usable
    gi = jnp.concatenate(gi, 0) * usable
    low = lax.rem(lax.broadcasted_iota(jnp.int32, (rows, width), 0), 2 * cg) < cg
    core = lax.rem(lax.axis_index("row"), 2)
    half = rows // 2
    for k in range(TAPS):
        s = acc_ref[k * rows : (k + 1) * rows]
        if k in PAIR_TAPS:
            i = TAPS + PAIR_TAPS.index(k)
            s = s + acc_ref[i * rows : (i + 1) * rows]
        other = jnp.where(low, pltpu.roll(s, rows - cg, 0), pltpu.roll(s, cg, 0))
        volts = gr * s + gi * other
        first, second = volts[:half], volts[half:]
        keep_ref[k] = jnp.where(core == 0, first, second)
        give_ref[k] = jnp.where(core == 0, second, first).astype(give_ref.dtype)


def front(samples, channel_index, gain_real, gain_imag, flags, groups):
    _, points, width = samples.shape
    channels = gain_real.shape[0]
    rows = 2 * channels
    depth = (TAPS + len(PAIR_TAPS)) * rows
    flags = flags.reshape(1, -1)
    return pl.pallas_call(
        functools.partial(front_body, groups=groups),
        name="front",
        out_shape=[
            jax.ShapeDtypeStruct((TAPS, rows // 2, width), jnp.float32),
            jax.ShapeDtypeStruct((TAPS, rows // 2, width), jnp.bfloat16),
        ],
        in_specs=[IN_HBM] * 5,
        out_specs=[IN_VMEM] * 2,
        scratch_shapes=[
            pltpu.SMEM(channel_index.shape, jnp.int32),
            pltpu.VMEM(gain_real.shape, jnp.float32),
            pltpu.VMEM(gain_imag.shape, jnp.float32),
            pltpu.VMEM(flags.shape, jnp.int32),
            pltpu.VMEM((points, width), samples.dtype),
            pltpu.VMEM((TAPS, points // LANES, LANES), jnp.float32),
            pltpu.VMEM((depth, points), jnp.bfloat16),
            pltpu.VMEM((depth, width), jnp.float32),
            pltpu.SemaphoreType.DMA((SPLITS,)),
            pltpu.SemaphoreType.DMA((4,)),
        ],
        compiler_params=pltpu.CompilerParams(vmem_limit_bytes=VMEM_BYTES),
    )(*in_hbm(channel_index, samples, gain_real, gain_imag, flags))


def pair_body(keep_ref, got_ref, here_ref, next_ref, after_ref):
    even = lax.rem(lax.axis_index("row"), 2) == 0
    half = keep_ref.shape[1]
    first, second = [], []
    for k in range(TAPS):
        keep, got = keep_ref[k], got_ref[k].astype(jnp.float32)
        first.append(jnp.where(even, keep, got))
        second.append(jnp.where(even, got, keep))
    here_ref[0] = first[3]
    here_ref[1] = first[2] + second[3]
    next_ref[:half] = (first[1] + second[2]).astype(next_ref.dtype)
    next_ref[half:] = (first[0] + second[1]).astype(next_ref.dtype)
    after_ref[...] = second[0].astype(after_ref.dtype)


def pair_sum(keep, got):
    _, half, width = keep.shape
    return pl.pallas_call(
        pair_body,
        name="pair_sum",
        out_shape=[
            jax.ShapeDtypeStruct((2, half, width), jnp.float32),
            jax.ShapeDtypeStruct((2 * half, width), jnp.bfloat16),
            jax.ShapeDtypeStruct((half, width), jnp.bfloat16),
        ],
        in_specs=[IN_VMEM] * 2,
        out_specs=[IN_VMEM] * 3,
        compiler_params=pltpu.CompilerParams(vmem_limit_bytes=VMEM_BYTES),
    )(keep, got)


def combine_body(here_ref, next_ref, after_ref, *refs):
    out_refs, total_ref = refs[:-1], refs[-1]
    groups, size, _ = total_ref.shape
    size = size // 2
    half = after_ref.shape[0]
    chip = lax.axis_index("tm") * (lax.axis_size("row") // 2) + lax.div(lax.axis_index("row"), 2)
    even = here_ref[0] + jnp.where(chip >= 1, next_ref[:half].astype(jnp.float32), 0.0)
    even = even + jnp.where(chip >= 2, after_ref[...].astype(jnp.float32), 0.0)
    odd = here_ref[1] + jnp.where(chip >= 1, next_ref[half:].astype(jnp.float32), 0.0)
    for g in range(groups):
        total_ref[g, :size] = even[g * size : (g + 1) * size]
        total_ref[g, size:] = odd[g * size : (g + 1) * size]
    me = lax.axis_index("chan")
    for j, ref in enumerate(out_refs):
        ref[...] = total_ref[lax.rem(me + j, groups)].astype(jnp.bfloat16)


def combine(here, following, after, groups):
    half, width = after.shape
    size = 2 * (half // groups)
    piece = jax.ShapeDtypeStruct((size, width), jnp.bfloat16)
    return pl.pallas_call(
        combine_body,
        name="combine",
        out_shape=[piece] * groups,
        in_specs=[IN_VMEM] * 3,
        out_specs=[IN_VMEM] * groups,
        scratch_shapes=[pltpu.VMEM((groups, size, width), jnp.float32)],
        compiler_params=pltpu.CompilerParams(vmem_limit_bytes=VMEM_BYTES),
    )(here, following, after)


def correlate_body(mine_ref, other_ref, out_ref, all_ref, left_ref, right_ref, tile_ref, sems, *, tile):
    chips, chunks, size, width = mine_ref.shape
    depth = chips * size
    size = size // 2
    cg = size // 2
    frames = 2 * chips
    rows, cols = out_ref.shape[2:]
    core = lax.rem(lax.axis_index("row"), 2)
    for ref, half in ((mine_ref, core), (other_ref, 1 - core)):
        for j in range(chunks):
            chunk = half * chunks + lax.rem(lax.axis_index("chan") + chunks - j, chunks)
            for m in range(chips):
                all_ref[chunk, m * 2 * size : (m + 1) * 2 * size, :] = ref[m, j].astype(jnp.float32)
    n_row, n_col = rows // width, cols // width
    lane = lax.broadcasted_iota(jnp.int32, (width, depth), 1)
    for q in range(n_row):
        turned = (all_ref[lax.axis_index("row") * n_row + q] * (1.0 / frames)).T
        for c in range(cg):
            mine = jnp.where(lax.rem(lane, cg) == c, turned, 0.0)
            left_ref[c, q * width : (q + 1) * width, :] = mine.astype(jnp.bfloat16)
    low = lax.rem(lax.broadcasted_iota(jnp.int32, (depth, width), 0), size) < cg
    for q in range(n_col):
        x = all_ref[lax.axis_index("tm") * n_col + q]
        part = slice(q * width, (q + 1) * width)
        right_ref[0, :, part] = x.astype(jnp.bfloat16)
        crossed = jnp.where(low, -pltpu.roll(x, depth - cg, 0), pltpu.roll(x, cg, 0))
        right_ref[1, :, part] = crossed.astype(jnp.bfloat16)

    high, wide = min(tile, rows), min(tile, cols)
    spots = [(top, left) for left in range(0, cols, wide) for top in range(0, rows, high)]
    total = 2 * cg

    def copy(n, s):
        top, left = spots[s]
        slot = lax.rem(n, 2)
        return pltpu.make_async_copy(
            tile_ref.at[slot, pl.ds(top, high), pl.ds(left, wide)],
            out_ref.at[lax.rem(n, 2), lax.div(n, 2), pl.ds(top, high), pl.ds(left, wide)],
            sems.at[slot, s],
        )

    def step(n, carry):
        @pl.when(n >= 2)
        def _():
            for s in range(len(spots)):
                copy(n - 2, s).wait()

        for s, (top, left) in enumerate(spots):
            product = jnp.dot(
                left_ref[lax.div(n, 2), top : top + high, :],
                right_ref[lax.rem(n, 2), :, left : left + wide],
                preferred_element_type=jnp.float32,
            )
            tile_ref[lax.rem(n, 2), top : top + high, left : left + wide] = product.astype(jnp.bfloat16)
            copy(n, s).start()
        return carry

    lax.fori_loop(0, total, step, 0)
    for n in range(total - 2, total):
        for s in range(len(spots)):
            copy(n, s).wait()


def correlate(mine, other, rows, cols):
    chips, chunks, size, width = mine.shape
    cg = size // 4
    depth = chips * size
    spots = (rows // min(TILE, rows)) * (cols // min(TILE, cols))
    return pl.pallas_call(
        functools.partial(correlate_body, tile=TILE),
        name="correlate",
        out_shape=jax.ShapeDtypeStruct((2, cg, rows, cols), jnp.bfloat16),
        in_specs=[IN_VMEM] * 2,
        out_specs=IN_HBM,
        scratch_shapes=[
            pltpu.VMEM((2 * chunks, depth, width), jnp.float32),
            pltpu.VMEM((cg, rows, depth), jnp.bfloat16),
            pltpu.VMEM((2, depth, cols), jnp.bfloat16),
            pltpu.VMEM((2, rows, cols), jnp.bfloat16),
            pltpu.SemaphoreType.DMA((2, spots)),
        ],
        compiler_params=pltpu.CompilerParams(vmem_limit_bytes=VMEM_BYTES),
    )(mine, other)


def turn_plane(value, by):
    planes, rows = lax.axis_size("chan"), lax.axis_size("row")
    half = planes // 2
    pairs = []
    for c in range(planes):
        for r in range(rows):
            to = (r % 2) * half + (c + by) % half
            pairs.append((c * rows + r, to * rows + r - r % 2 + c // half))
    return lax.ppermute(value, ("chan", "row"), pairs)


def swapped(value):
    peers = lax.axis_size(FRAME_AXES)
    return lax.ppermute(value, FRAME_AXES, [(i, i ^ 1) for i in range(peers)])


def local(samples, channel_index, gain_real, gain_imag, flags):
    planes = lax.axis_size("chan")
    chips = lax.axis_size(FRAME_AXES) // 2
    inputs_total = samples.shape[2] * planes
    keep, give = front(samples, channel_index, gain_real, gain_imag, flags, planes)
    here, following, after = pair_sum(keep, swapped(give))
    following = rotated(following, FRAME_AXES, 2)
    after = rotated(after, FRAME_AXES, 4)
    pieces = combine(here, following, after, planes // 2)
    pieces = jnp.stack([turn_plane(piece, j) for j, piece in enumerate(pieces)])
    mine = jnp.stack([pieces] + [rotated(pieces, FRAME_AXES, 2 * s) for s in range(1, chips)])
    return correlate(mine, swapped(mine), inputs_total // lax.axis_size("row"), inputs_total // lax.axis_size("tm"))


def solution(mesh):
    in_specs = (P(("tm", "row"), None, "chan"), P(), P(None, "chan"), P(None, "chan"), P("chan"))
    out_specs = P(None, "chan", "row", "tm")
    return jax.shard_map(local, mesh=mesh, in_specs=in_specs, out_specs=out_specs, check_vma=False)
```

```python
import functools
import math

import jax
import jax.numpy as jnp
from jax import lax
from jax.experimental import pallas as pl
from jax.experimental.pallas import tpu as pltpu
from jax.sharding import PartitionSpec as P

TAPS = 4
LANES = 128
PAIR_TAPS = (1, 2)
SPLITS = 8
TILE = 512
VMEM_BYTES = 48 << 20
FRAME_AXES = ("tm", "row")

IN_VMEM = pl.BlockSpec(memory_space=pltpu.VMEM)
IN_HBM = pl.BlockSpec(memory_space=pltpu.HBM)


def in_hbm(*arrays):
    return [pltpu.with_memory_space_constraint(a, pltpu.HBM) for a in arrays]


def rotated(value, axis, by):
    peers = lax.axis_size(axis)
    return lax.ppermute(value, axis, [(i, (i + by) % peers) for i in range(peers)])


def plane_steps(planes):
    assert planes & (planes - 1) == 0 and planes > 1
    steps = [[], []]
    for step in reversed(range(planes)):
        steps[bin(step).count("1") % 2].append(step)
    return steps


def sine_quarter(x):
    y = x * x
    acc = 1.0 / 6227020800.0
    for k in (-1.0 / 39916800.0, 1.0 / 362880.0, -1.0 / 5040.0, 1.0 / 120.0, -1.0 / 6.0, 1.0):
        acc = acc * y + k
    return acc * x


def turn(m, quarter):
    q = (m + quarter // 2) >> (quarter.bit_length() - 1)
    r = (m - q * quarter).astype(jnp.float32) * (math.pi / 2 / quarter)
    y = r * r
    cos = ((((-1.0 / 3628800.0 * y + 1.0 / 40320.0) * y - 1.0 / 720.0) * y + 1.0 / 24.0) * y - 0.5) * y + 1.0
    sin = ((((1.0 / 362880.0 * y - 1.0 / 5040.0) * y + 1.0 / 120.0) * y - 1.0 / 6.0) * y + 1.0) * r
    odd = (q & 1) == 1
    first = jnp.where(odd, sin, cos)
    second = jnp.where(odd, cos, sin)
    return jnp.where(((q + 1) & 2) != 0, -first, first), jnp.where((q & 2) != 0, -second, second)


def front_body(
    index_hbm, samples_ref, gr_hbm, gi_hbm, flags_hbm,
    keep_ref, give_ref,
    index_ref, gr_ref, gi_ref, flags_ref, block_ref, filter_ref, table_ref, acc_ref, group_ref, sems, small_sems,
    *, groups,
):
    points, width = block_ref.shape
    channels = gr_ref.shape[0]
    cg = channels // groups
    rows = 2 * channels
    quarter = points // 4
    index_copy = pltpu.make_async_copy(index_hbm, index_ref, small_sems.at[0])
    index_copy.start()
    part = points // SPLITS
    fetches = [
        pltpu.make_async_copy(
            samples_ref.at[0, pl.ds(i * part, part), :], block_ref.at[pl.ds(i * part, part), :], sems.at[i]
        )
        for i in range(SPLITS)
    ]
    for copy in fetches:
        copy.start()
    others = [
        pltpu.make_async_copy(src, dst, small_sems.at[1 + i])
        for i, (src, dst) in enumerate(((gr_hbm, gr_ref), (gi_hbm, gi_ref), (flags_hbm, flags_ref)))
    ]
    for copy in others:
        copy.start()

    spans = points // LANES
    at = lax.broadcasted_iota(jnp.int32, (spans, LANES), 0) * LANES
    at = at + lax.broadcasted_iota(jnp.int32, (spans, LANES), 1)
    u = (at.astype(jnp.float32) + 0.5) * (1.0 / points)
    sn = sine_quarter(u * (math.pi / 2))
    cs = sine_quarter((1.0 - u) * (math.pi / 2))
    sp = 2.0 * sn * cs * (1.0 / math.pi / math.sqrt(points))
    filter_ref[0] = sp / (u - 2.0) * (0.5 - 0.5 * cs)
    filter_ref[1] = -sp / (u - 1.0) * (0.5 + 0.5 * sn)
    filter_ref[2] = sp / u * (0.5 + 0.5 * cs)
    filter_ref[3] = -sp / (u + 1.0) * (0.5 - 0.5 * sn)

    rho = lax.broadcasted_iota(jnp.int32, (rows, LANES), 0)
    lane = lax.broadcasted_iota(jnp.int32, (rows, LANES), 1)
    chan = lax.div(rho, 2 * cg) * cg + lax.rem(rho, cg)
    imag = jnp.where(lax.rem(rho, 2 * cg) >= cg, quarter, 0)
    index_copy.wait()
    index = jnp.zeros((rows, LANES), jnp.int32)
    for c in range(channels):
        index = jnp.where(chan == c, index_ref[c], index)
    cos_a, sin_a = turn(index * lane + imag, quarter)
    cos_b, sin_b = turn(index * lane * LANES, quarter)
    for a in range(spans):
        v = cos_a * cos_b[:, a : a + 1] - sin_a * sin_b[:, a : a + 1]
        cols = slice(a * LANES, (a + 1) * LANES)
        for k in range(TAPS):
            t = filter_ref[k, a : a + 1, :] * v
            high = t.astype(jnp.bfloat16)
            table_ref[k * rows : (k + 1) * rows, cols] = high
            if k in PAIR_TAPS:
                i = TAPS + PAIR_TAPS.index(k)
                table_ref[i * rows : (i + 1) * rows, cols] = (t - high.astype(jnp.float32)).astype(jnp.bfloat16)
    for i, copy in enumerate(fetches):
        copy.wait()
        span = slice(i * part, (i + 1) * part)
        product = jnp.dot(table_ref[:, span], block_ref[span, :], preferred_element_type=jnp.float32)
        acc_ref[...] = product if i == 0 else acc_ref[...] + product

    for copy in others:
        copy.wait()
    row = lax.broadcasted_iota(jnp.int32, (LANES, 2 * LANES), 0)
    col = lax.broadcasted_iota(jnp.int32, (LANES, 2 * LANES), 1)
    spread = jnp.where(row == lax.div(col, 2), 1.0, 0.0).astype(jnp.bfloat16)
    usable = []
    for j in range(flags_ref.shape[1] // LANES):
        some = flags_ref[:, j * LANES : (j + 1) * LANES].astype(jnp.float32)
        some = jnp.broadcast_to(some, (8, LANES)).astype(jnp.bfloat16)
        usable.append(jnp.dot(some, spread, preferred_element_type=jnp.float32))
    usable = usable[0] if len(usable) == 1 else jnp.concatenate(usable, 1)
    usable = jnp.concatenate([usable] * (rows // 8), 0)
    gr, gi = [], []
    for g in range(groups):
        a, b = gr_ref[g * cg : (g + 1) * cg], gi_ref[g * cg : (g + 1) * cg]
        gr += [a, a]
        gi += [-b, b]
    gr = jnp.concatenate(gr, 0) * usable
    gi = jnp.concatenate(gi, 0) * usable
    low = lax.rem(lax.broadcasted_iota(jnp.int32, (rows, width), 0), 2 * cg) < cg
    core, plane = lax.rem(lax.axis_index("row"), 2), lax.axis_index("chan")
    steps = plane_steps(groups)
    size = 2 * cg
    for k in range(TAPS):
        s = acc_ref[k * rows : (k + 1) * rows]
        if k in PAIR_TAPS:
            i = TAPS + PAIR_TAPS.index(k)
            s = s + acc_ref[i * rows : (i + 1) * rows]
        other = jnp.where(low, pltpu.roll(s, rows - cg, 0), pltpu.roll(s, cg, 0))
        volts = gr * s + gi * other
        for g in range(groups):
            group_ref[g] = volts[g * size : (g + 1) * size]
        for i in range(groups // 2):
            even, odd = group_ref[plane ^ steps[0][i]], group_ref[plane ^ steps[1][i]]
            keep_ref[k, i * size : (i + 1) * size] = jnp.where(core == 0, even, odd)
            give_ref[k, i * size : (i + 1) * size] = jnp.where(core == 0, odd, even).astype(give_ref.dtype)


def front(samples, channel_index, gain_real, gain_imag, flags, groups):
    _, points, width = samples.shape
    channels = gain_real.shape[0]
    rows = 2 * channels
    depth = (TAPS + len(PAIR_TAPS)) * rows
    flags = flags.reshape(1, -1)
    return pl.pallas_call(
        functools.partial(front_body, groups=groups),
        name="front",
        out_shape=[
            jax.ShapeDtypeStruct((TAPS, rows // 2, width), jnp.float32),
            jax.ShapeDtypeStruct((TAPS, rows // 2, width), jnp.bfloat16),
        ],
        in_specs=[IN_HBM] * 5,
        out_specs=[IN_VMEM] * 2,
        scratch_shapes=[
            pltpu.SMEM(channel_index.shape, jnp.int32),
            pltpu.VMEM(gain_real.shape, jnp.float32),
            pltpu.VMEM(gain_imag.shape, jnp.float32),
            pltpu.VMEM(flags.shape, jnp.int32),
            pltpu.VMEM((points, width), samples.dtype),
            pltpu.VMEM((TAPS, points // LANES, LANES), jnp.float32),
            pltpu.VMEM((depth, points), jnp.bfloat16),
            pltpu.VMEM((depth, width), jnp.float32),
            pltpu.VMEM((groups, rows // groups, width), jnp.float32),
            pltpu.SemaphoreType.DMA((SPLITS,)),
            pltpu.SemaphoreType.DMA((4,)),
        ],
        compiler_params=pltpu.CompilerParams(vmem_limit_bytes=VMEM_BYTES),
    )(*in_hbm(channel_index, samples, gain_real, gain_imag, flags))


def pair_body(keep_ref, got_ref, here_ref, next_ref, after_ref):
    even = lax.rem(lax.axis_index("row"), 2) == 0
    half = keep_ref.shape[1]
    first, second = [], []
    for k in range(TAPS):
        keep, got = keep_ref[k], got_ref[k].astype(jnp.float32)
        first.append(jnp.where(even, keep, got))
        second.append(jnp.where(even, got, keep))
    here_ref[0] = first[3]
    here_ref[1] = first[2] + second[3]
    next_ref[:half] = (first[1] + second[2]).astype(next_ref.dtype)
    next_ref[half:] = (first[0] + second[1]).astype(next_ref.dtype)
    after_ref[...] = second[0].astype(after_ref.dtype)


def pair_sum(keep, got):
    _, half, width = keep.shape
    return pl.pallas_call(
        pair_body,
        name="pair_sum",
        out_shape=[
            jax.ShapeDtypeStruct((2, half, width), jnp.float32),
            jax.ShapeDtypeStruct((2 * half, width), jnp.bfloat16),
            jax.ShapeDtypeStruct((half, width), jnp.bfloat16),
        ],
        in_specs=[IN_VMEM] * 2,
        out_specs=[IN_VMEM] * 3,
        compiler_params=pltpu.CompilerParams(vmem_limit_bytes=VMEM_BYTES),
    )(keep, got)


def combine_body(here_ref, next_ref, after_ref, *refs):
    out_refs, total_ref = refs[:-1], refs[-1]
    size = total_ref.shape[0] // 2
    half = after_ref.shape[0]
    chip = lax.axis_index("tm") * (lax.axis_size("row") // 2) + lax.div(lax.axis_index("row"), 2)
    even = here_ref[0] + jnp.where(chip >= 1, next_ref[:half].astype(jnp.float32), 0.0)
    even = even + jnp.where(chip >= 2, after_ref[...].astype(jnp.float32), 0.0)
    odd = here_ref[1] + jnp.where(chip >= 1, next_ref[half:].astype(jnp.float32), 0.0)
    for g, ref in enumerate(out_refs):
        total_ref[:size] = even[g * size : (g + 1) * size]
        total_ref[size:] = odd[g * size : (g + 1) * size]
        ref[...] = total_ref[...].astype(jnp.bfloat16)


def combine(here, following, after, groups):
    half, width = after.shape
    size = 2 * (half // groups)
    piece = jax.ShapeDtypeStruct((size, width), jnp.bfloat16)
    return pl.pallas_call(
        combine_body,
        name="combine",
        out_shape=[piece] * groups,
        in_specs=[IN_VMEM] * 3,
        out_specs=[IN_VMEM] * groups,
        scratch_shapes=[pltpu.VMEM((size, width), jnp.float32)],
        compiler_params=pltpu.CompilerParams(vmem_limit_bytes=VMEM_BYTES),
    )(here, following, after)


def correlate_body(mine_ref, other_ref, out_ref, all_ref, left_ref, right_ref, tile_ref, sems, *, tile):
    chips, chunks, size, width = mine_ref.shape
    depth = chips * size
    size = size // 2
    cg = size // 2
    frames = 2 * chips
    rows, cols = out_ref.shape[2:]
    core = lax.rem(lax.axis_index("row"), 2)
    steps = plane_steps(2 * chunks)
    for ref, half in ((mine_ref, core), (other_ref, 1 - core)):
        for j in range(chunks):
            chunk = lax.axis_index("chan") ^ jnp.where(half == 0, steps[0][j], steps[1][j])
            for m in range(chips):
                all_ref[chunk, m * 2 * size : (m + 1) * 2 * size, :] = ref[m, j].astype(jnp.float32)
    n_row, n_col = rows // width, cols // width
    lane = lax.broadcasted_iota(jnp.int32, (width, depth), 1)
    for q in range(n_row):
        turned = (all_ref[lax.axis_index("row") * n_row + q] * (1.0 / frames)).T
        for c in range(cg):
            mine = jnp.where(lax.rem(lane, cg) == c, turned, 0.0)
            left_ref[c, q * width : (q + 1) * width, :] = mine.astype(jnp.bfloat16)
    low = lax.rem(lax.broadcasted_iota(jnp.int32, (depth, width), 0), size) < cg
    for q in range(n_col):
        x = all_ref[lax.axis_index("tm") * n_col + q]
        part = slice(q * width, (q + 1) * width)
        right_ref[0, :, part] = x.astype(jnp.bfloat16)
        crossed = jnp.where(low, -pltpu.roll(x, depth - cg, 0), pltpu.roll(x, cg, 0))
        right_ref[1, :, part] = crossed.astype(jnp.bfloat16)

    high, wide = min(tile, rows), min(tile, cols)
    spots = [(top, left) for left in range(0, cols, wide) for top in range(0, rows, high)]
    total = 2 * cg

    def copy(n, s):
        top, left = spots[s]
        slot = lax.rem(n, 2)
        return pltpu.make_async_copy(
            tile_ref.at[slot, pl.ds(top, high), pl.ds(left, wide)],
            out_ref.at[lax.rem(n, 2), lax.div(n, 2), pl.ds(top, high), pl.ds(left, wide)],
            sems.at[slot, s],
        )

    def step(n, carry):
        @pl.when(n >= 2)
        def _():
            for s in range(len(spots)):
                copy(n - 2, s).wait()

        for s, (top, left) in enumerate(spots):
            product = jnp.dot(
                left_ref[lax.div(n, 2), top : top + high, :],
                right_ref[lax.rem(n, 2), :, left : left + wide],
                preferred_element_type=jnp.float32,
            )
            tile_ref[lax.rem(n, 2), top : top + high, left : left + wide] = product.astype(jnp.bfloat16)
            copy(n, s).start()
        return carry

    lax.fori_loop(0, total, step, 0)
    for n in range(total - 2, total):
        for s in range(len(spots)):
            copy(n, s).wait()


def correlate(mine, other, rows, cols):
    chips, chunks, size, width = mine.shape
    cg = size // 4
    depth = chips * size
    spots = (rows // min(TILE, rows)) * (cols // min(TILE, cols))
    return pl.pallas_call(
        functools.partial(correlate_body, tile=TILE),
        name="correlate",
        out_shape=jax.ShapeDtypeStruct((2, cg, rows, cols), jnp.bfloat16),
        in_specs=[IN_VMEM] * 2,
        out_specs=IN_HBM,
        scratch_shapes=[
            pltpu.VMEM((2 * chunks, depth, width), jnp.float32),
            pltpu.VMEM((cg, rows, depth), jnp.bfloat16),
            pltpu.VMEM((2, depth, cols), jnp.bfloat16),
            pltpu.VMEM((2, rows, cols), jnp.bfloat16),
            pltpu.SemaphoreType.DMA((2, spots)),
        ],
        compiler_params=pltpu.CompilerParams(vmem_limit_bytes=VMEM_BYTES),
    )(mine, other)


def turn_plane(value, i):
    planes, rows = lax.axis_size("chan"), lax.axis_size("row")
    steps = plane_steps(planes)
    pairs = [(c * rows + r, (c ^ steps[r % 2][i]) * rows + r) for c in range(planes) for r in range(rows)]
    return lax.ppermute(value, ("chan", "row"), pairs)


def swapped(value):
    peers = lax.axis_size(FRAME_AXES)
    return lax.ppermute(value, FRAME_AXES, [(i, i ^ 1) for i in range(peers)])


def local(samples, channel_index, gain_real, gain_imag, flags):
    planes = lax.axis_size("chan")
    chips = lax.axis_size(FRAME_AXES) // 2
    inputs_total = samples.shape[2] * planes
    keep, give = front(samples, channel_index, gain_real, gain_imag, flags, planes)
    here, following, after = pair_sum(keep, swapped(give))
    following = rotated(following, FRAME_AXES, 2)
    after = rotated(after, FRAME_AXES, 4)
    pieces = combine(here, following, after, planes // 2)
    pieces = jnp.stack([turn_plane(piece, j) for j, piece in enumerate(pieces)])
    peers = 2 * chips
    mine = jnp.stack([pieces] + [lax.ppermute(pieces, FRAME_AXES, [(i, i ^ (2 * s)) for i in range(peers)]) for s in range(1, chips)])
    return correlate(mine, swapped(mine), inputs_total // lax.axis_size("row"), inputs_total // lax.axis_size("tm"))


def solution(mesh):
    in_specs = (P(("tm", "row"), None, "chan"), P(), P(None, "chan"), P(None, "chan"), P("chan"))
    out_specs = P(None, "chan", "row", "tm")
    return jax.shard_map(local, mesh=mesh, in_specs=in_specs, out_specs=out_specs, check_vma=False)
```

```python
import functools
import math

import jax
import jax.numpy as jnp
from jax import lax
from jax.experimental import pallas as pl
from jax.experimental.pallas import tpu as pltpu
from jax.sharding import PartitionSpec as P

TAPS = 4
LANES = 128
PAIR_TAPS = (1, 2)
SPLITS = 8
TILE = 512
VMEM_BYTES = 48 << 20
FRAME_AXES = ("tm", "row")

IN_VMEM = pl.BlockSpec(memory_space=pltpu.VMEM)
IN_HBM = pl.BlockSpec(memory_space=pltpu.HBM)


def in_hbm(*arrays):
    return [pltpu.with_memory_space_constraint(a, pltpu.HBM) for a in arrays]


def rotated(value, axis, by):
    peers = lax.axis_size(axis)
    return lax.ppermute(value, axis, [(i, (i + by) % peers) for i in range(peers)])


def plane_steps(planes):
    assert planes & (planes - 1) == 0 and planes > 1
    steps = [[], []]
    for step in reversed(range(planes)):
        steps[bin(step).count("1") % 2].append(step)
    return steps


def chunk_of(plane, core, i, steps):
    even, odd = steps[0][i], steps[1][i]
    return plane ^ jnp.where(((core ^ plane ^ even) & 1) == 0, even, odd)


def sine_quarter(x):
    y = x * x
    acc = 1.0 / 6227020800.0
    for k in (-1.0 / 39916800.0, 1.0 / 362880.0, -1.0 / 5040.0, 1.0 / 120.0, -1.0 / 6.0, 1.0):
        acc = acc * y + k
    return acc * x


def turn(m, quarter):
    q = (m + quarter // 2) >> (quarter.bit_length() - 1)
    r = (m - q * quarter).astype(jnp.float32) * (math.pi / 2 / quarter)
    y = r * r
    cos = ((((-1.0 / 3628800.0 * y + 1.0 / 40320.0) * y - 1.0 / 720.0) * y + 1.0 / 24.0) * y - 0.5) * y + 1.0
    sin = ((((1.0 / 362880.0 * y - 1.0 / 5040.0) * y + 1.0 / 120.0) * y - 1.0 / 6.0) * y + 1.0) * r
    odd = (q & 1) == 1
    first = jnp.where(odd, sin, cos)
    second = jnp.where(odd, cos, sin)
    return jnp.where(((q + 1) & 2) != 0, -first, first), jnp.where((q & 2) != 0, -second, second)


def front_body(
    index_hbm, samples_ref, gr_hbm, gi_hbm, flags_hbm,
    keep_ref, give_ref,
    index_ref, gr_ref, gi_ref, flags_ref, block_ref, filter_ref, table_ref, acc_ref, group_ref, sems, small_sems,
    *, groups,
):
    points, width = block_ref.shape
    channels = gr_ref.shape[0]
    cg = channels // groups
    rows = 2 * channels
    quarter = points // 4
    index_copy = pltpu.make_async_copy(index_hbm, index_ref, small_sems.at[0])
    index_copy.start()
    part = points // SPLITS
    fetches = [
        pltpu.make_async_copy(
            samples_ref.at[0, pl.ds(i * part, part), :], block_ref.at[pl.ds(i * part, part), :], sems.at[i]
        )
        for i in range(SPLITS)
    ]
    for copy in fetches:
        copy.start()
    others = [
        pltpu.make_async_copy(src, dst, small_sems.at[1 + i])
        for i, (src, dst) in enumerate(((gr_hbm, gr_ref), (gi_hbm, gi_ref), (flags_hbm, flags_ref)))
    ]
    for copy in others:
        copy.start()

    spans = points // LANES
    at = lax.broadcasted_iota(jnp.int32, (spans, LANES), 0) * LANES
    at = at + lax.broadcasted_iota(jnp.int32, (spans, LANES), 1)
    u = (at.astype(jnp.float32) + 0.5) * (1.0 / points)
    sn = sine_quarter(u * (math.pi / 2))
    cs = sine_quarter((1.0 - u) * (math.pi / 2))
    sp = 2.0 * sn * cs * (1.0 / math.pi / math.sqrt(points))
    filter_ref[0] = sp / (u - 2.0) * (0.5 - 0.5 * cs)
    filter_ref[1] = -sp / (u - 1.0) * (0.5 + 0.5 * sn)
    filter_ref[2] = sp / u * (0.5 + 0.5 * cs)
    filter_ref[3] = -sp / (u + 1.0) * (0.5 - 0.5 * sn)

    rho = lax.broadcasted_iota(jnp.int32, (rows, LANES), 0)
    lane = lax.broadcasted_iota(jnp.int32, (rows, LANES), 1)
    chan = lax.div(rho, 2 * cg) * cg + lax.rem(rho, cg)
    imag = jnp.where(lax.rem(rho, 2 * cg) >= cg, quarter, 0)
    index_copy.wait()
    index = jnp.zeros((rows, LANES), jnp.int32)
    for c in range(channels):
        index = jnp.where(chan == c, index_ref[c], index)
    cos_a, sin_a = turn(index * lane + imag, quarter)
    cos_b, sin_b = turn(index * lane * LANES, quarter)
    for a in range(spans):
        v = cos_a * cos_b[:, a : a + 1] - sin_a * sin_b[:, a : a + 1]
        cols = slice(a * LANES, (a + 1) * LANES)
        for k in range(TAPS):
            t = filter_ref[k, a : a + 1, :] * v
            high = t.astype(jnp.bfloat16)
            table_ref[k * rows : (k + 1) * rows, cols] = high
            if k in PAIR_TAPS:
                i = TAPS + PAIR_TAPS.index(k)
                table_ref[i * rows : (i + 1) * rows, cols] = (t - high.astype(jnp.float32)).astype(jnp.bfloat16)
    for i, copy in enumerate(fetches):
        copy.wait()
        span = slice(i * part, (i + 1) * part)
        product = jnp.dot(table_ref[:, span], block_ref[span, :], preferred_element_type=jnp.float32)
        acc_ref[...] = product if i == 0 else acc_ref[...] + product

    for copy in others:
        copy.wait()
    row = lax.broadcasted_iota(jnp.int32, (LANES, 2 * LANES), 0)
    col = lax.broadcasted_iota(jnp.int32, (LANES, 2 * LANES), 1)
    spread = jnp.where(row == lax.div(col, 2), 1.0, 0.0).astype(jnp.bfloat16)
    usable = []
    for j in range(flags_ref.shape[1] // LANES):
        some = flags_ref[:, j * LANES : (j + 1) * LANES].astype(jnp.float32)
        some = jnp.broadcast_to(some, (8, LANES)).astype(jnp.bfloat16)
        usable.append(jnp.dot(some, spread, preferred_element_type=jnp.float32))
    usable = usable[0] if len(usable) == 1 else jnp.concatenate(usable, 1)
    usable = jnp.concatenate([usable] * (rows // 8), 0)
    gr, gi = [], []
    for g in range(groups):
        a, b = gr_ref[g * cg : (g + 1) * cg], gi_ref[g * cg : (g + 1) * cg]
        gr += [a, a]
        gi += [-b, b]
    gr = jnp.concatenate(gr, 0) * usable
    gi = jnp.concatenate(gi, 0) * usable
    low = lax.rem(lax.broadcasted_iota(jnp.int32, (rows, width), 0), 2 * cg) < cg
    core, plane = lax.rem(lax.axis_index("row"), 2), lax.axis_index("chan")
    steps = plane_steps(groups)
    size = 2 * cg
    for k in range(TAPS):
        s = acc_ref[k * rows : (k + 1) * rows]
        if k in PAIR_TAPS:
            i = TAPS + PAIR_TAPS.index(k)
            s = s + acc_ref[i * rows : (i + 1) * rows]
        other = jnp.where(low, pltpu.roll(s, rows - cg, 0), pltpu.roll(s, cg, 0))
        volts = gr * s + gi * other
        for g in range(groups):
            group_ref[g] = volts[g * size : (g + 1) * size]
        for i in range(groups // 2):
            even, odd = group_ref[plane ^ steps[0][i]], group_ref[plane ^ steps[1][i]]
            keep_ref[k, i * size : (i + 1) * size] = jnp.where(core == 0, even, odd)
            give_ref[k, i * size : (i + 1) * size] = jnp.where(core == 0, odd, even).astype(give_ref.dtype)


def front(samples, channel_index, gain_real, gain_imag, flags, groups):
    _, points, width = samples.shape
    channels = gain_real.shape[0]
    rows = 2 * channels
    depth = (TAPS + len(PAIR_TAPS)) * rows
    flags = flags.reshape(1, -1)
    return pl.pallas_call(
        functools.partial(front_body, groups=groups),
        name="front",
        out_shape=[
            jax.ShapeDtypeStruct((TAPS, rows // 2, width), jnp.float32),
            jax.ShapeDtypeStruct((TAPS, rows // 2, width), jnp.bfloat16),
        ],
        in_specs=[IN_HBM] * 5,
        out_specs=[IN_VMEM] * 2,
        scratch_shapes=[
            pltpu.SMEM(channel_index.shape, jnp.int32),
            pltpu.VMEM(gain_real.shape, jnp.float32),
            pltpu.VMEM(gain_imag.shape, jnp.float32),
            pltpu.VMEM(flags.shape, jnp.int32),
            pltpu.VMEM((points, width), samples.dtype),
            pltpu.VMEM((TAPS, points // LANES, LANES), jnp.float32),
            pltpu.VMEM((depth, points), jnp.bfloat16),
            pltpu.VMEM((depth, width), jnp.float32),
            pltpu.VMEM((groups, rows // groups, width), jnp.float32),
            pltpu.SemaphoreType.DMA((SPLITS,)),
            pltpu.SemaphoreType.DMA((4,)),
        ],
        compiler_params=pltpu.CompilerParams(vmem_limit_bytes=VMEM_BYTES),
    )(*in_hbm(channel_index, samples, gain_real, gain_imag, flags))


def pair_body(keep_ref, got_ref, here_ref, next_ref, after_ref):
    even = lax.rem(lax.axis_index("row"), 2) == 0
    half = keep_ref.shape[1]
    first, second = [], []
    for k in range(TAPS):
        keep, got = keep_ref[k], got_ref[k].astype(jnp.float32)
        first.append(jnp.where(even, keep, got))
        second.append(jnp.where(even, got, keep))
    here_ref[0] = first[3]
    here_ref[1] = first[2] + second[3]
    next_ref[:half] = (first[1] + second[2]).astype(next_ref.dtype)
    next_ref[half:] = (first[0] + second[1]).astype(next_ref.dtype)
    after_ref[...] = second[0].astype(after_ref.dtype)


def pair_sum(keep, got):
    _, half, width = keep.shape
    return pl.pallas_call(
        pair_body,
        name="pair_sum",
        out_shape=[
            jax.ShapeDtypeStruct((2, half, width), jnp.float32),
            jax.ShapeDtypeStruct((2 * half, width), jnp.bfloat16),
            jax.ShapeDtypeStruct((half, width), jnp.bfloat16),
        ],
        in_specs=[IN_VMEM] * 2,
        out_specs=[IN_VMEM] * 3,
        compiler_params=pltpu.CompilerParams(vmem_limit_bytes=VMEM_BYTES),
    )(keep, got)


def combine_body(here_ref, next_ref, after_ref, *refs):
    out_refs, total_ref = refs[:-1], refs[-1]
    size = total_ref.shape[0] // 2
    half = after_ref.shape[0]
    chip = lax.axis_index("tm") * (lax.axis_size("row") // 2) + lax.div(lax.axis_index("row"), 2)
    even = here_ref[0] + jnp.where(chip >= 1, next_ref[:half].astype(jnp.float32), 0.0)
    even = even + jnp.where(chip >= 2, after_ref[...].astype(jnp.float32), 0.0)
    odd = here_ref[1] + jnp.where(chip >= 1, next_ref[half:].astype(jnp.float32), 0.0)
    for g, ref in enumerate(out_refs):
        total_ref[:size] = even[g * size : (g + 1) * size]
        total_ref[size:] = odd[g * size : (g + 1) * size]
        ref[...] = total_ref[...].astype(jnp.bfloat16)


def combine(here, following, after, groups):
    half, width = after.shape
    size = 2 * (half // groups)
    piece = jax.ShapeDtypeStruct((size, width), jnp.bfloat16)
    return pl.pallas_call(
        combine_body,
        name="combine",
        out_shape=[piece] * groups,
        in_specs=[IN_VMEM] * 3,
        out_specs=[IN_VMEM] * groups,
        scratch_shapes=[pltpu.VMEM((size, width), jnp.float32)],
        compiler_params=pltpu.CompilerParams(vmem_limit_bytes=VMEM_BYTES),
    )(here, following, after)


def correlate_body(*refs, phase, tile):
    mine_ref, other_ref = refs[0], refs[1]
    out_ref, all_ref, left_ref, right_ref, tile_ref, sems = refs[-6:]
    chips, chunks, size, width = mine_ref.shape
    depth = chips * size
    size = size // 2
    cg = size // 2
    frames = 2 * chips
    rows = out_ref.shape[2]
    cols = tile_ref.shape[3]
    core, plane = lax.rem(lax.axis_index("row"), 2), lax.axis_index("chan")
    steps = plane_steps(2 * chunks)
    for ref, half in ((mine_ref, core),) + (() if phase == 0 else ((other_ref, 1 - core),)):
        for j in range(chunks):
            chunk = chunk_of(plane, half, j, steps)
            for m in range(chips):
                all_ref[chunk, m * 2 * size : (m + 1) * 2 * size, :] = ref[m, j].astype(jnp.float32)
    n_row, n_col = rows // width, cols // width
    lane = lax.broadcasted_iota(jnp.int32, (width, depth), 1)
    for q in range(n_row):
        turned = (all_ref[lax.axis_index("row") * n_row + q] * (1.0 / frames)).T
        for c in range(cg):
            mine = jnp.where(lax.rem(lane, cg) == c, turned, 0.0)
            left_ref[c, q * width : (q + 1) * width, :] = mine.astype(jnp.bfloat16)
    shift = {None: 0, 0: core, 1: 1 - core}[phase]
    first = lax.axis_index("tm") * (out_ref.shape[3] // width) + shift
    low = lax.rem(lax.broadcasted_iota(jnp.int32, (depth, width), 0), size) < cg
    for q in range(n_col):
        x = all_ref[first + q]
        part = slice(q * width, (q + 1) * width)
        right_ref[0, :, part] = x.astype(jnp.bfloat16)
        crossed = jnp.where(low, -pltpu.roll(x, depth - cg, 0), pltpu.roll(x, cg, 0))
        right_ref[1, :, part] = crossed.astype(jnp.bfloat16)

    high, wide = min(tile, rows), min(tile, cols)
    spots = [(top, left) for left in range(0, cols, wide) for top in range(0, rows, high)]

    slots = tile_ref.shape[0]

    def copy(ri, c, s):
        top, left = spots[s]
        slot = c % slots
        return pltpu.make_async_copy(
            tile_ref.at[slot, ri, pl.ds(top, high), pl.ds(left, wide)],
            out_ref.at[ri, c, pl.ds(top, high), pl.ds(pl.multiple_of(shift * width + left, wide), wide)],
            sems.at[slot, ri, s],
        )

    def step(c, carry):
        if c >= slots:
            for ri in range(2):
                for s in range(len(spots)):
                    copy(ri, c - slots, s).wait()

        for ri in range(2):
            for s, (top, left) in enumerate(spots):
                product = jnp.dot(
                    left_ref[c, top : top + high, :],
                    right_ref[ri, :, left : left + wide],
                    preferred_element_type=jnp.float32,
                )
                tile_ref[c % slots, ri, top : top + high, left : left + wide] = product.astype(jnp.bfloat16)
                copy(ri, c, s).start()

    for c in range(cg):
        step(c, 0)
    for c in range(max(cg - slots, 0), cg):
        for ri in range(2):
            for s in range(len(spots)):
                copy(ri, c, s).wait()


def correlate(operands, rows, cols, phase):
    chips, chunks, size, width = operands[0].shape
    cg = size // 4
    depth = chips * size
    span = cols if phase is None else width
    spots = (rows // min(TILE, rows)) * (span // min(TILE, span))
    return pl.pallas_call(
        functools.partial(correlate_body, phase=phase, tile=TILE),
        name="correlate" if phase is None else ("correlate_near", "correlate_far")[phase],
        out_shape=jax.ShapeDtypeStruct((2, cg, rows, cols), jnp.bfloat16),
        in_specs=[IN_VMEM] * min(len(operands), 2) + [IN_HBM] * (len(operands) - 2),
        out_specs=IN_HBM,
        input_output_aliases={2: 0} if phase == 1 else {},
        scratch_shapes=[
            pltpu.VMEM((2 * chunks, depth, width), jnp.float32),
            pltpu.VMEM((cg, rows, depth), jnp.bfloat16),
            pltpu.VMEM((2, depth, span), jnp.bfloat16),
            pltpu.VMEM((2, 2, rows, span), jnp.bfloat16),
            pltpu.SemaphoreType.DMA((2, 2, spots)),
        ],
        compiler_params=pltpu.CompilerParams(vmem_limit_bytes=VMEM_BYTES),
    )(*operands)


def turn_plane(value, i):
    planes, rows = lax.axis_size("chan"), lax.axis_size("row")
    steps = plane_steps(planes)
    pairs = []
    for c in range(planes):
        for r in range(rows):
            pairs.append((c * rows + r, (c ^ steps[r % 2][i]) * rows + r - r % 2 + c % 2))
    return lax.ppermute(value, ("chan", "row"), pairs)


def swapped(value):
    peers = lax.axis_size(FRAME_AXES)
    return lax.ppermute(value, FRAME_AXES, [(i, i ^ 1) for i in range(peers)])


def local(samples, channel_index, gain_real, gain_imag, flags):
    planes = lax.axis_size("chan")
    chips = lax.axis_size(FRAME_AXES) // 2
    inputs_total = samples.shape[2] * planes
    keep, give = front(samples, channel_index, gain_real, gain_imag, flags, planes)
    here, following, after = pair_sum(keep, swapped(give))
    after = rotated(after, FRAME_AXES, 4)
    following = rotated(following, FRAME_AXES, 2)
    pieces = combine(here, following, after, planes // 2)
    pieces = jnp.stack([turn_plane(piece, j) for j, piece in enumerate(pieces)])
    peers = 2 * chips
    mine = jnp.stack([pieces] + [lax.ppermute(pieces, FRAME_AXES, [(i, i ^ (2 * s)) for i in range(peers)]) for s in range(1, chips)])
    other = swapped(mine)
    rows, cols = inputs_total // lax.axis_size("row"), inputs_total // lax.axis_size("tm")
    width = samples.shape[2]
    if rows != width or cols != 2 * width:
        return correlate([mine, other], rows, cols, None)
    near = correlate([mine], rows, cols, 0)
    return correlate([mine, other, near], rows, cols, 1)


def solution(mesh):
    in_specs = (P(("tm", "row"), None, "chan"), P(), P(None, "chan"), P(None, "chan"), P("chan"))
    out_specs = P(None, "chan", "row", "tm")
    return jax.shard_map(local, mesh=mesh, in_specs=in_specs, out_specs=out_specs, check_vma=False)
```

```python
import functools
import math

import jax
import jax.numpy as jnp
from jax import lax
from jax.experimental import pallas as pl
from jax.experimental.pallas import tpu as pltpu
from jax.sharding import PartitionSpec as P

TAPS = 4
LANES = 128
PAIR_TAPS = (1, 2)
SPLITS = 8
TILE = 512
VMEM_BYTES = 48 << 20
FRAME_AXES = ("tm", "row")

IN_VMEM = pl.BlockSpec(memory_space=pltpu.VMEM)
IN_HBM = pl.BlockSpec(memory_space=pltpu.HBM)


def in_hbm(*arrays):
    return [pltpu.with_memory_space_constraint(a, pltpu.HBM) for a in arrays]


def rotated(value, axis, by):
    peers = lax.axis_size(axis)
    return lax.ppermute(value, axis, [(i, (i + by) % peers) for i in range(peers)])


def plane_steps(planes):
    assert planes & (planes - 1) == 0 and planes > 1
    steps = [[], []]
    for step in reversed(range(planes)):
        steps[bin(step).count("1") % 2].append(step)
    return steps


def chunk_of(plane, core, i, steps):
    even, odd = steps[0][i], steps[1][i]
    return plane ^ jnp.where(((core ^ plane ^ even) & 1) == 0, even, odd)


def sine_quarter(x):
    y = x * x
    acc = 1.0 / 6227020800.0
    for k in (-1.0 / 39916800.0, 1.0 / 362880.0, -1.0 / 5040.0, 1.0 / 120.0, -1.0 / 6.0, 1.0):
        acc = acc * y + k
    return acc * x


def turn(m, quarter):
    q = (m + quarter // 2) >> (quarter.bit_length() - 1)
    r = (m - q * quarter).astype(jnp.float32) * (math.pi / 2 / quarter)
    y = r * r
    cos = ((((-1.0 / 3628800.0 * y + 1.0 / 40320.0) * y - 1.0 / 720.0) * y + 1.0 / 24.0) * y - 0.5) * y + 1.0
    sin = ((((1.0 / 362880.0 * y - 1.0 / 5040.0) * y + 1.0 / 120.0) * y - 1.0 / 6.0) * y + 1.0) * r
    odd = (q & 1) == 1
    first = jnp.where(odd, sin, cos)
    second = jnp.where(odd, cos, sin)
    return jnp.where(((q + 1) & 2) != 0, -first, first), jnp.where((q & 2) != 0, -second, second)


def front_body(
    index_hbm, samples_ref, gr_hbm, gi_hbm, flags_hbm,
    keep_ref, give_ref,
    index_ref, gr_ref, gi_ref, flags_ref, block_ref, filter_ref, table_ref, acc_ref, group_ref, sems, small_sems,
    *, groups,
):
    points, width = block_ref.shape
    channels = gr_ref.shape[0]
    cg = channels // groups
    rows = 2 * channels
    quarter = points // 4
    index_copy = pltpu.make_async_copy(index_hbm, index_ref, small_sems.at[0])
    index_copy.start()
    part = points // SPLITS
    fetches = [
        pltpu.make_async_copy(
            samples_ref.at[0, pl.ds(i * part, part), :], block_ref.at[pl.ds(i * part, part), :], sems.at[i]
        )
        for i in range(SPLITS)
    ]
    for copy in fetches:
        copy.start()
    others = [
        pltpu.make_async_copy(src, dst, small_sems.at[1 + i])
        for i, (src, dst) in enumerate(((gr_hbm, gr_ref), (gi_hbm, gi_ref), (flags_hbm, flags_ref)))
    ]
    for copy in others:
        copy.start()

    spans = points // LANES
    at = lax.broadcasted_iota(jnp.int32, (spans, LANES), 0) * LANES
    at = at + lax.broadcasted_iota(jnp.int32, (spans, LANES), 1)
    u = (at.astype(jnp.float32) + 0.5) * (1.0 / points)
    sn = sine_quarter(u * (math.pi / 2))
    cs = sine_quarter((1.0 - u) * (math.pi / 2))
    sp = 2.0 * sn * cs * (1.0 / math.pi / math.sqrt(points))
    filter_ref[0] = sp / (u - 2.0) * (0.5 - 0.5 * cs)
    filter_ref[1] = -sp / (u - 1.0) * (0.5 + 0.5 * sn)
    filter_ref[2] = sp / u * (0.5 + 0.5 * cs)
    filter_ref[3] = -sp / (u + 1.0) * (0.5 - 0.5 * sn)

    rho = lax.broadcasted_iota(jnp.int32, (rows, LANES), 0)
    lane = lax.broadcasted_iota(jnp.int32, (rows, LANES), 1)
    chan = lax.div(rho, 2 * cg) * cg + lax.rem(rho, cg)
    imag = jnp.where(lax.rem(rho, 2 * cg) >= cg, quarter, 0)
    index_copy.wait()
    index = jnp.zeros((rows, LANES), jnp.int32)
    for c in range(channels):
        index = jnp.where(chan == c, index_ref[c], index)
    cos_a, sin_a = turn(index * lane + imag, quarter)
    cos_b, sin_b = turn(index * lane * LANES, quarter)
    for a in range(spans):
        v = cos_a * cos_b[:, a : a + 1] - sin_a * sin_b[:, a : a + 1]
        cols = slice(a * LANES, (a + 1) * LANES)
        for k in range(TAPS):
            t = filter_ref[k, a : a + 1, :] * v
            high = t.astype(jnp.bfloat16)
            table_ref[k * rows : (k + 1) * rows, cols] = high
            if k in PAIR_TAPS:
                i = TAPS + PAIR_TAPS.index(k)
                table_ref[i * rows : (i + 1) * rows, cols] = (t - high.astype(jnp.float32)).astype(jnp.bfloat16)
    for i, copy in enumerate(fetches):
        copy.wait()
        span = slice(i * part, (i + 1) * part)
        product = jnp.dot(table_ref[:, span], block_ref[span, :], preferred_element_type=jnp.float32)
        acc_ref[...] = product if i == 0 else acc_ref[...] + product

    for copy in others:
        copy.wait()
    row = lax.broadcasted_iota(jnp.int32, (LANES, 2 * LANES), 0)
    col = lax.broadcasted_iota(jnp.int32, (LANES, 2 * LANES), 1)
    spread = jnp.where(row == lax.div(col, 2), 1.0, 0.0).astype(jnp.bfloat16)
    usable = []
    for j in range(flags_ref.shape[1] // LANES):
        some = flags_ref[:, j * LANES : (j + 1) * LANES].astype(jnp.float32)
        some = jnp.broadcast_to(some, (8, LANES)).astype(jnp.bfloat16)
        usable.append(jnp.dot(some, spread, preferred_element_type=jnp.float32))
    usable = usable[0] if len(usable) == 1 else jnp.concatenate(usable, 1)
    usable = jnp.concatenate([usable] * (rows // 8), 0)
    gr, gi = [], []
    for g in range(groups):
        a, b = gr_ref[g * cg : (g + 1) * cg], gi_ref[g * cg : (g + 1) * cg]
        gr += [a, a]
        gi += [-b, b]
    gr = jnp.concatenate(gr, 0) * usable
    gi = jnp.concatenate(gi, 0) * usable
    low = lax.rem(lax.broadcasted_iota(jnp.int32, (rows, width), 0), 2 * cg) < cg
    core, plane = lax.rem(lax.axis_index("row"), 2), lax.axis_index("chan")
    steps = plane_steps(groups)
    size = 2 * cg
    for k in range(TAPS):
        s = acc_ref[k * rows : (k + 1) * rows]
        if k in PAIR_TAPS:
            i = TAPS + PAIR_TAPS.index(k)
            s = s + acc_ref[i * rows : (i + 1) * rows]
        other = jnp.where(low, pltpu.roll(s, rows - cg, 0), pltpu.roll(s, cg, 0))
        volts = gr * s + gi * other
        for g in range(groups):
            group_ref[g] = volts[g * size : (g + 1) * size]
        for i in range(groups // 2):
            even, odd = group_ref[plane ^ steps[0][i]], group_ref[plane ^ steps[1][i]]
            keep_ref[k, i * size : (i + 1) * size] = jnp.where(core == 0, even, odd)
            give_ref[k, i * size : (i + 1) * size] = jnp.where(core == 0, odd, even).astype(give_ref.dtype)


def front(samples, channel_index, gain_real, gain_imag, flags, groups):
    _, points, width = samples.shape
    channels = gain_real.shape[0]
    rows = 2 * channels
    depth = (TAPS + len(PAIR_TAPS)) * rows
    flags = flags.reshape(1, -1)
    return pl.pallas_call(
        functools.partial(front_body, groups=groups),
        name="front",
        out_shape=[
            jax.ShapeDtypeStruct((TAPS, rows // 2, width), jnp.float32),
            jax.ShapeDtypeStruct((TAPS, rows // 2, width), jnp.bfloat16),
        ],
        in_specs=[IN_HBM] * 5,
        out_specs=[IN_VMEM] * 2,
        scratch_shapes=[
            pltpu.SMEM(channel_index.shape, jnp.int32),
            pltpu.VMEM(gain_real.shape, jnp.float32),
            pltpu.VMEM(gain_imag.shape, jnp.float32),
            pltpu.VMEM(flags.shape, jnp.int32),
            pltpu.VMEM((points, width), samples.dtype),
            pltpu.VMEM((TAPS, points // LANES, LANES), jnp.float32),
            pltpu.VMEM((depth, points), jnp.bfloat16),
            pltpu.VMEM((depth, width), jnp.float32),
            pltpu.VMEM((groups, rows // groups, width), jnp.float32),
            pltpu.SemaphoreType.DMA((SPLITS,)),
            pltpu.SemaphoreType.DMA((4,)),
        ],
        compiler_params=pltpu.CompilerParams(vmem_limit_bytes=VMEM_BYTES),
    )(*in_hbm(channel_index, samples, gain_real, gain_imag, flags))


def pair_body(keep_ref, got_ref, here_ref, next_ref, after_ref):
    even = lax.rem(lax.axis_index("row"), 2) == 0
    half = keep_ref.shape[1]
    first, second = [], []
    for k in range(TAPS):
        keep, got = keep_ref[k], got_ref[k].astype(jnp.float32)
        first.append(jnp.where(even, keep, got))
        second.append(jnp.where(even, got, keep))
    here_ref[0] = first[3]
    here_ref[1] = first[2] + second[3]
    next_ref[:half] = (first[1] + second[2]).astype(next_ref.dtype)
    next_ref[half:] = (first[0] + second[1]).astype(next_ref.dtype)
    after_ref[...] = second[0].astype(after_ref.dtype)


def pair_sum(keep, got):
    _, half, width = keep.shape
    return pl.pallas_call(
        pair_body,
        name="pair_sum",
        out_shape=[
            jax.ShapeDtypeStruct((2, half, width), jnp.float32),
            jax.ShapeDtypeStruct((2 * half, width), jnp.bfloat16),
            jax.ShapeDtypeStruct((half, width), jnp.bfloat16),
        ],
        in_specs=[IN_VMEM] * 2,
        out_specs=[IN_VMEM] * 3,
        compiler_params=pltpu.CompilerParams(vmem_limit_bytes=VMEM_BYTES),
    )(keep, got)


def combine_body(here_ref, next_ref, after_ref, *refs):
    out_refs, total_ref = refs[:-1], refs[-1]
    size = total_ref.shape[0] // 2
    half = after_ref.shape[0]
    chip = lax.axis_index("tm") * (lax.axis_size("row") // 2) + lax.div(lax.axis_index("row"), 2)
    even = here_ref[0] + jnp.where(chip >= 1, next_ref[:half].astype(jnp.float32), 0.0)
    even = even + jnp.where(chip >= 2, after_ref[...].astype(jnp.float32), 0.0)
    odd = here_ref[1] + jnp.where(chip >= 1, next_ref[half:].astype(jnp.float32), 0.0)
    for g, ref in enumerate(out_refs):
        total_ref[:size] = even[g * size : (g + 1) * size]
        total_ref[size:] = odd[g * size : (g + 1) * size]
        ref[...] = total_ref[...].astype(jnp.bfloat16)


def combine(here, following, after, groups):
    half, width = after.shape
    size = 2 * (half // groups)
    piece = jax.ShapeDtypeStruct((size, width), jnp.bfloat16)
    return pl.pallas_call(
        combine_body,
        name="combine",
        out_shape=[piece] * groups,
        in_specs=[IN_VMEM] * 3,
        out_specs=[IN_VMEM] * groups,
        scratch_shapes=[pltpu.VMEM((size, width), jnp.float32)],
        compiler_params=pltpu.CompilerParams(vmem_limit_bytes=VMEM_BYTES),
    )(here, following, after)


def correlate_body(*refs, phase, tile):
    mine_ref, other_ref = refs[0], refs[1]
    out_ref, all_ref, left_ref, right_ref, tile_ref, sems = refs[-6:]
    chips, chunks, size, width = mine_ref.shape
    depth = chips * size
    size = size // 2
    cg = size // 2
    frames = 2 * chips
    rows = out_ref.shape[2]
    cols = tile_ref.shape[3]
    core, plane = lax.rem(lax.axis_index("row"), 2), lax.axis_index("chan")
    steps = plane_steps(2 * chunks)
    for ref, half in ((mine_ref, core),) + (() if phase == 0 else ((other_ref, 1 - core),)):
        for j in range(chunks):
            chunk = chunk_of(plane, half, j, steps)
            for m in range(chips):
                all_ref[chunk, m * 2 * size : (m + 1) * 2 * size, :] = ref[m, j].astype(jnp.float32)
    n_row, n_col = rows // width, cols // width
    lane = lax.broadcasted_iota(jnp.int32, (width, depth), 1)
    turned = [(all_ref[lax.axis_index("row") * n_row + q] * (1.0 / frames)).T for q in range(n_row)]

    def set_left(c):
        for q in range(n_row):
            mine = jnp.where(lax.rem(lane, cg) == c, turned[q], 0.0)
            left_ref[c, q * width : (q + 1) * width, :] = mine.astype(jnp.bfloat16)

    shift = {None: 0, 0: core, 1: 1 - core}[phase]
    first = lax.axis_index("tm") * (out_ref.shape[3] // width) + shift
    low = lax.rem(lax.broadcasted_iota(jnp.int32, (depth, width), 0), size) < cg

    def set_right(ri):
        for q in range(n_col):
            x = all_ref[first + q]
            if ri == 1:
                x = jnp.where(low, -pltpu.roll(x, depth - cg, 0), pltpu.roll(x, cg, 0))
            right_ref[ri, :, q * width : (q + 1) * width] = x.astype(jnp.bfloat16)

    high, wide = min(tile, rows), min(tile, cols)
    spots = [(top, left) for left in range(0, cols, wide) for top in range(0, rows, high)]

    slots = tile_ref.shape[0]

    def copy(ri, c, s):
        top, left = spots[s]
        slot = c % slots
        return pltpu.make_async_copy(
            tile_ref.at[slot, ri, pl.ds(top, high), pl.ds(left, wide)],
            out_ref.at[ri, c, pl.ds(top, high), pl.ds(pl.multiple_of(shift * width + left, wide), wide)],
            sems.at[slot, ri, s],
        )

    def step(c, carry):
        if c >= slots:
            for ri in range(2):
                for s in range(len(spots)):
                    copy(ri, c - slots, s).wait()

        set_left(c)
        for ri in range(2):
            if c == 0:
                set_right(ri)
            for s, (top, left) in enumerate(spots):
                product = jnp.dot(
                    left_ref[c, top : top + high, :],
                    right_ref[ri, :, left : left + wide],
                    preferred_element_type=jnp.float32,
                )
                tile_ref[c % slots, ri, top : top + high, left : left + wide] = product.astype(jnp.bfloat16)
                copy(ri, c, s).start()

    for c in range(cg):
        step(c, 0)
    for c in range(max(cg - slots, 0), cg):
        for ri in range(2):
            for s in range(len(spots)):
                copy(ri, c, s).wait()


def correlate(operands, rows, cols, phase):
    chips, chunks, size, width = operands[0].shape
    cg = size // 4
    depth = chips * size
    span = cols if phase is None else width
    spots = (rows // min(TILE, rows)) * (span // min(TILE, span))
    return pl.pallas_call(
        functools.partial(correlate_body, phase=phase, tile=TILE),
        name="correlate" if phase is None else ("correlate_near", "correlate_far")[phase],
        out_shape=jax.ShapeDtypeStruct((2, cg, rows, cols), jnp.bfloat16),
        in_specs=[IN_VMEM] * min(len(operands), 2) + [IN_HBM] * (len(operands) - 2),
        out_specs=IN_HBM,
        input_output_aliases={2: 0} if phase == 1 else {},
        scratch_shapes=[
            pltpu.VMEM((2 * chunks, depth, width), jnp.float32),
            pltpu.VMEM((cg, rows, depth), jnp.bfloat16),
            pltpu.VMEM((2, depth, span), jnp.bfloat16),
            pltpu.VMEM((2, 2, rows, span), jnp.bfloat16),
            pltpu.SemaphoreType.DMA((2, 2, spots)),
        ],
        compiler_params=pltpu.CompilerParams(vmem_limit_bytes=VMEM_BYTES),
    )(*operands)


def turn_plane(value, i):
    planes, rows = lax.axis_size("chan"), lax.axis_size("row")
    steps = plane_steps(planes)
    pairs = []
    for c in range(planes):
        for r in range(rows):
            pairs.append((c * rows + r, (c ^ steps[r % 2][i]) * rows + r - r % 2 + c % 2))
    return lax.ppermute(value, ("chan", "row"), pairs)


def swapped(value):
    peers = lax.axis_size(FRAME_AXES)
    return lax.ppermute(value, FRAME_AXES, [(i, i ^ 1) for i in range(peers)])


def local(samples, channel_index, gain_real, gain_imag, flags):
    planes = lax.axis_size("chan")
    chips = lax.axis_size(FRAME_AXES) // 2
    inputs_total = samples.shape[2] * planes
    keep, give = front(samples, channel_index, gain_real, gain_imag, flags, planes)
    here, following, after = pair_sum(keep, swapped(give))
    after = rotated(after, FRAME_AXES, 4)
    following = rotated(following, FRAME_AXES, 2)
    pieces = combine(here, following, after, planes // 2)
    pieces = jnp.stack([turn_plane(piece, j) for j, piece in enumerate(pieces)])
    peers = 2 * chips
    mine = jnp.stack([pieces] + [lax.ppermute(pieces, FRAME_AXES, [(i, i ^ (2 * s)) for i in range(peers)]) for s in range(1, chips)])
    other = swapped(mine)
    rows, cols = inputs_total // lax.axis_size("row"), inputs_total // lax.axis_size("tm")
    width = samples.shape[2]
    if rows != width or cols != 2 * width:
        return correlate([mine, other], rows, cols, None)
    near = correlate([mine], rows, cols, 0)
    return correlate([mine, other, near], rows, cols, 1)


def solution(mesh):
    in_specs = (P(("tm", "row"), None, "chan"), P(), P(None, "chan"), P(None, "chan"), P("chan"))
    out_specs = P(None, "chan", "row", "tm")
    return jax.shard_map(local, mesh=mesh, in_specs=in_specs, out_specs=out_specs, check_vma=False)
```

```python
import functools
import math

import jax
import jax.numpy as jnp
from jax import lax
from jax.experimental import pallas as pl
from jax.experimental.pallas import tpu as pltpu
from jax.sharding import PartitionSpec as P

TAPS = 4
LANES = 128
PAIR_TAPS = (1, 2)
SHARES = (3, 3, 3, 3, 2, 1, 1)
TILE = 512
VMEM_BYTES = 48 << 20
FRAME_AXES = ("tm", "row")

IN_VMEM = pl.BlockSpec(memory_space=pltpu.VMEM)
IN_HBM = pl.BlockSpec(memory_space=pltpu.HBM)


def in_hbm(*arrays):
    return [pltpu.with_memory_space_constraint(a, pltpu.HBM) for a in arrays]


def rotated(value, axis, by):
    peers = lax.axis_size(axis)
    return lax.ppermute(value, axis, [(i, (i + by) % peers) for i in range(peers)])


def plane_steps(planes):
    assert planes & (planes - 1) == 0 and planes > 1
    steps = [[], []]
    for step in reversed(range(planes)):
        steps[bin(step).count("1") % 2].append(step)
    return steps


def chunk_of(plane, core, i, steps):
    even, odd = steps[0][i], steps[1][i]
    return plane ^ jnp.where(((core ^ plane ^ even) & 1) == 0, even, odd)


def sine_quarter(x):
    y = x * x
    acc = 1.0 / 6227020800.0
    for k in (-1.0 / 39916800.0, 1.0 / 362880.0, -1.0 / 5040.0, 1.0 / 120.0, -1.0 / 6.0, 1.0):
        acc = acc * y + k
    return acc * x


def turn(m, quarter):
    q = (m + quarter // 2) >> (quarter.bit_length() - 1)
    r = (m - q * quarter).astype(jnp.float32) * (math.pi / 2 / quarter)
    y = r * r
    cos = ((((-1.0 / 3628800.0 * y + 1.0 / 40320.0) * y - 1.0 / 720.0) * y + 1.0 / 24.0) * y - 0.5) * y + 1.0
    sin = ((((1.0 / 362880.0 * y - 1.0 / 5040.0) * y + 1.0 / 120.0) * y - 1.0 / 6.0) * y + 1.0) * r
    odd = (q & 1) == 1
    first = jnp.where(odd, sin, cos)
    second = jnp.where(odd, cos, sin)
    return jnp.where(((q + 1) & 2) != 0, -first, first), jnp.where((q & 2) != 0, -second, second)


def front_body(
    index_hbm, samples_ref, gr_hbm, gi_hbm, flags_hbm,
    keep_ref, give_ref,
    index_ref, gr_ref, gi_ref, flags_ref, block_ref, filter_ref, table_ref, acc_ref, group_ref, sems, small_sems,
    *, groups,
):
    points, width = block_ref.shape
    channels = gr_ref.shape[0]
    cg = channels // groups
    rows = 2 * channels
    quarter = points // 4
    index_copy = pltpu.make_async_copy(index_hbm, index_ref, small_sems.at[0])
    index_copy.start()
    edges = [points * sum(SHARES[:i]) // sum(SHARES) for i in range(len(SHARES) + 1)]
    pieces = list(zip(edges, edges[1:]))
    fetches = [
        pltpu.make_async_copy(
            samples_ref.at[0, pl.ds(lo, hi - lo), :], block_ref.at[pl.ds(lo, hi - lo), :], sems.at[i]
        )
        for i, (lo, hi) in enumerate(pieces)
    ]
    for copy in fetches:
        copy.start()
    others = [
        pltpu.make_async_copy(src, dst, small_sems.at[1 + i])
        for i, (src, dst) in enumerate(((gr_hbm, gr_ref), (gi_hbm, gi_ref), (flags_hbm, flags_ref)))
    ]
    for copy in others:
        copy.start()

    spans = points // LANES
    at = lax.broadcasted_iota(jnp.int32, (spans, LANES), 0) * LANES
    at = at + lax.broadcasted_iota(jnp.int32, (spans, LANES), 1)
    u = (at.astype(jnp.float32) + 0.5) * (1.0 / points)
    sn = sine_quarter(u * (math.pi / 2))
    cs = sine_quarter((1.0 - u) * (math.pi / 2))
    sp = 2.0 * sn * cs * (1.0 / math.pi / math.sqrt(points))
    filter_ref[0] = sp / (u - 2.0) * (0.5 - 0.5 * cs)
    filter_ref[1] = -sp / (u - 1.0) * (0.5 + 0.5 * sn)
    filter_ref[2] = sp / u * (0.5 + 0.5 * cs)
    filter_ref[3] = -sp / (u + 1.0) * (0.5 - 0.5 * sn)

    rho = lax.broadcasted_iota(jnp.int32, (rows, LANES), 0)
    lane = lax.broadcasted_iota(jnp.int32, (rows, LANES), 1)
    chan = lax.div(rho, 2 * cg) * cg + lax.rem(rho, cg)
    imag = jnp.where(lax.rem(rho, 2 * cg) >= cg, quarter, 0)
    index_copy.wait()
    index = jnp.zeros((rows, LANES), jnp.int32)
    for c in range(channels):
        index = jnp.where(chan == c, index_ref[c], index)
    cos_a, sin_a = turn(index * lane + imag, quarter)
    cos_b, sin_b = turn(index * lane * LANES, quarter)
    for a in range(spans):
        v = cos_a * cos_b[:, a : a + 1] - sin_a * sin_b[:, a : a + 1]
        cols = slice(a * LANES, (a + 1) * LANES)
        for k in range(TAPS):
            t = filter_ref[k, a : a + 1, :] * v
            high = t.astype(jnp.bfloat16)
            table_ref[k * rows : (k + 1) * rows, cols] = high
            if k in PAIR_TAPS:
                i = TAPS + PAIR_TAPS.index(k)
                table_ref[i * rows : (i + 1) * rows, cols] = (t - high.astype(jnp.float32)).astype(jnp.bfloat16)
    for i, copy in enumerate(fetches):
        copy.wait()
        span = slice(*pieces[i])
        product = jnp.dot(table_ref[:, span], block_ref[span, :], preferred_element_type=jnp.float32)
        acc_ref[...] = product if i == 0 else acc_ref[...] + product

    for copy in others:
        copy.wait()
    row = lax.broadcasted_iota(jnp.int32, (LANES, 2 * LANES), 0)
    col = lax.broadcasted_iota(jnp.int32, (LANES, 2 * LANES), 1)
    spread = jnp.where(row == lax.div(col, 2), 1.0, 0.0).astype(jnp.bfloat16)
    usable = []
    for j in range(flags_ref.shape[1] // LANES):
        some = flags_ref[:, j * LANES : (j + 1) * LANES].astype(jnp.float32)
        some = jnp.broadcast_to(some, (8, LANES)).astype(jnp.bfloat16)
        usable.append(jnp.dot(some, spread, preferred_element_type=jnp.float32))
    usable = usable[0] if len(usable) == 1 else jnp.concatenate(usable, 1)
    usable = jnp.concatenate([usable] * (rows // 8), 0)
    gr, gi = [], []
    for g in range(groups):
        a, b = gr_ref[g * cg : (g + 1) * cg], gi_ref[g * cg : (g + 1) * cg]
        gr += [a, a]
        gi += [-b, b]
    gr = jnp.concatenate(gr, 0) * usable
    gi = jnp.concatenate(gi, 0) * usable
    low = lax.rem(lax.broadcasted_iota(jnp.int32, (rows, width), 0), 2 * cg) < cg
    core, plane = lax.rem(lax.axis_index("row"), 2), lax.axis_index("chan")
    steps = plane_steps(groups)
    size = 2 * cg
    for k in range(TAPS):
        s = acc_ref[k * rows : (k + 1) * rows]
        if k in PAIR_TAPS:
            i = TAPS + PAIR_TAPS.index(k)
            s = s + acc_ref[i * rows : (i + 1) * rows]
        other = jnp.where(low, pltpu.roll(s, rows - cg, 0), pltpu.roll(s, cg, 0))
        volts = gr * s + gi * other
        for g in range(groups):
            group_ref[g] = volts[g * size : (g + 1) * size]
        for i in range(groups // 2):
            even, odd = group_ref[plane ^ steps[0][i]], group_ref[plane ^ steps[1][i]]
            keep_ref[k, i * size : (i + 1) * size] = jnp.where(core == 0, even, odd)
            give_ref[k, i * size : (i + 1) * size] = jnp.where(core == 0, odd, even).astype(give_ref.dtype)


def front(samples, channel_index, gain_real, gain_imag, flags, groups):
    _, points, width = samples.shape
    channels = gain_real.shape[0]
    rows = 2 * channels
    depth = (TAPS + len(PAIR_TAPS)) * rows
    flags = flags.reshape(1, -1)
    return pl.pallas_call(
        functools.partial(front_body, groups=groups),
        name="front",
        out_shape=[
            jax.ShapeDtypeStruct((TAPS, rows // 2, width), jnp.float32),
            jax.ShapeDtypeStruct((TAPS, rows // 2, width), jnp.bfloat16),
        ],
        in_specs=[IN_HBM] * 5,
        out_specs=[IN_VMEM] * 2,
        scratch_shapes=[
            pltpu.SMEM(channel_index.shape, jnp.int32),
            pltpu.VMEM(gain_real.shape, jnp.float32),
            pltpu.VMEM(gain_imag.shape, jnp.float32),
            pltpu.VMEM(flags.shape, jnp.int32),
            pltpu.VMEM((points, width), samples.dtype),
            pltpu.VMEM((TAPS, points // LANES, LANES), jnp.float32),
            pltpu.VMEM((depth, points), jnp.bfloat16),
            pltpu.VMEM((depth, width), jnp.float32),
            pltpu.VMEM((groups, rows // groups, width), jnp.float32),
            pltpu.SemaphoreType.DMA((len(SHARES),)),
            pltpu.SemaphoreType.DMA((4,)),
        ],
        compiler_params=pltpu.CompilerParams(vmem_limit_bytes=VMEM_BYTES),
    )(*in_hbm(channel_index, samples, gain_real, gain_imag, flags))


def pair_body(keep_ref, got_ref, here_ref, next_ref, after_ref):
    even = lax.rem(lax.axis_index("row"), 2) == 0
    half = keep_ref.shape[1]
    first, second = [], []
    for k in range(TAPS):
        keep, got = keep_ref[k], got_ref[k].astype(jnp.float32)
        first.append(jnp.where(even, keep, got))
        second.append(jnp.where(even, got, keep))
    here_ref[0] = first[3]
    here_ref[1] = first[2] + second[3]
    next_ref[:half] = (first[1] + second[2]).astype(next_ref.dtype)
    next_ref[half:] = (first[0] + second[1]).astype(next_ref.dtype)
    after_ref[...] = second[0].astype(after_ref.dtype)


def pair_sum(keep, got):
    _, half, width = keep.shape
    return pl.pallas_call(
        pair_body,
        name="pair_sum",
        out_shape=[
            jax.ShapeDtypeStruct((2, half, width), jnp.float32),
            jax.ShapeDtypeStruct((2 * half, width), jnp.bfloat16),
            jax.ShapeDtypeStruct((half, width), jnp.bfloat16),
        ],
        in_specs=[IN_VMEM] * 2,
        out_specs=[IN_VMEM] * 3,
        compiler_params=pltpu.CompilerParams(vmem_limit_bytes=VMEM_BYTES),
    )(keep, got)


def combine_body(here_ref, next_ref, after_ref, *refs):
    out_refs, total_ref = refs[:-1], refs[-1]
    size = total_ref.shape[0] // 2
    half = after_ref.shape[0]
    chip = lax.axis_index("tm") * (lax.axis_size("row") // 2) + lax.div(lax.axis_index("row"), 2)
    even = here_ref[0] + jnp.where(chip >= 1, next_ref[:half].astype(jnp.float32), 0.0)
    even = even + jnp.where(chip >= 2, after_ref[...].astype(jnp.float32), 0.0)
    odd = here_ref[1] + jnp.where(chip >= 1, next_ref[half:].astype(jnp.float32), 0.0)
    for g, ref in enumerate(out_refs):
        total_ref[:size] = even[g * size : (g + 1) * size]
        total_ref[size:] = odd[g * size : (g + 1) * size]
        ref[...] = total_ref[...].astype(jnp.bfloat16)


def combine(here, following, after, groups):
    half, width = after.shape
    size = 2 * (half // groups)
    piece = jax.ShapeDtypeStruct((size, width), jnp.bfloat16)
    return pl.pallas_call(
        combine_body,
        name="combine",
        out_shape=[piece] * groups,
        in_specs=[IN_VMEM] * 3,
        out_specs=[IN_VMEM] * groups,
        scratch_shapes=[pltpu.VMEM((size, width), jnp.float32)],
        compiler_params=pltpu.CompilerParams(vmem_limit_bytes=VMEM_BYTES),
    )(here, following, after)


def correlate_body(*refs, phase, tile):
    mine_ref, other_ref = refs[0], refs[1]
    out_ref, all_ref, left_ref, right_ref, tile_ref, sems = refs[-6:]
    chips, chunks, size, width = mine_ref.shape
    depth = chips * size
    size = size // 2
    cg = size // 2
    frames = 2 * chips
    rows = out_ref.shape[2]
    cols = tile_ref.shape[3]
    core, plane = lax.rem(lax.axis_index("row"), 2), lax.axis_index("chan")
    steps = plane_steps(2 * chunks)
    for ref, half in ((mine_ref, core),) + (() if phase == 0 else ((other_ref, 1 - core),)):
        for j in range(chunks):
            chunk = chunk_of(plane, half, j, steps)
            for m in range(chips):
                all_ref[chunk, m * 2 * size : (m + 1) * 2 * size, :] = ref[m, j].astype(jnp.float32)
    n_row, n_col = rows // width, cols // width
    lane = lax.broadcasted_iota(jnp.int32, (width, depth), 1)
    turned = [(all_ref[lax.axis_index("row") * n_row + q] * (1.0 / frames)).T for q in range(n_row)]

    def set_left(c):
        for q in range(n_row):
            mine = jnp.where(lax.rem(lane, cg) == c, turned[q], 0.0)
            left_ref[c, q * width : (q + 1) * width, :] = mine.astype(jnp.bfloat16)

    shift = {None: 0, 0: core, 1: 1 - core}[phase]
    first = lax.axis_index("tm") * (out_ref.shape[3] // width) + shift
    low = lax.rem(lax.broadcasted_iota(jnp.int32, (depth, width), 0), size) < cg

    def set_right(ri):
        for q in range(n_col):
            x = all_ref[first + q]
            if ri == 1:
                x = jnp.where(low, -pltpu.roll(x, depth - cg, 0), pltpu.roll(x, cg, 0))
            right_ref[ri, :, q * width : (q + 1) * width] = x.astype(jnp.bfloat16)

    high, wide = min(tile, rows), min(tile, cols)
    spots = [(top, left) for left in range(0, cols, wide) for top in range(0, rows, high)]

    slots = tile_ref.shape[0]

    def copy(ri, c, s):
        top, left = spots[s]
        slot = c % slots
        return pltpu.make_async_copy(
            tile_ref.at[slot, ri, pl.ds(top, high), pl.ds(left, wide)],
            out_ref.at[ri, c, pl.ds(top, high), pl.ds(pl.multiple_of(shift * width + left, wide), wide)],
            sems.at[slot, ri, s],
        )

    def step(c, carry):
        if c >= slots:
            for ri in range(2):
                for s in range(len(spots)):
                    copy(ri, c - slots, s).wait()

        set_left(c)
        for ri in range(2):
            if c == 0:
                set_right(ri)
            for s, (top, left) in enumerate(spots):
                product = jnp.dot(
                    left_ref[c, top : top + high, :],
                    right_ref[ri, :, left : left + wide],
                    preferred_element_type=jnp.float32,
                )
                tile_ref[c % slots, ri, top : top + high, left : left + wide] = product.astype(jnp.bfloat16)
                copy(ri, c, s).start()

    for c in range(cg):
        step(c, 0)
    for c in range(max(cg - slots, 0), cg):
        for ri in range(2):
            for s in range(len(spots)):
                copy(ri, c, s).wait()


def correlate(operands, rows, cols, phase):
    chips, chunks, size, width = operands[0].shape
    cg = size // 4
    depth = chips * size
    span = cols if phase is None else width
    spots = (rows // min(TILE, rows)) * (span // min(TILE, span))
    return pl.pallas_call(
        functools.partial(correlate_body, phase=phase, tile=TILE),
        name="correlate" if phase is None else ("correlate_near", "correlate_far")[phase],
        out_shape=jax.ShapeDtypeStruct((2, cg, rows, cols), jnp.bfloat16),
        in_specs=[IN_VMEM] * min(len(operands), 2) + [IN_HBM] * (len(operands) - 2),
        out_specs=IN_HBM,
        input_output_aliases={2: 0} if phase == 1 else {},
        scratch_shapes=[
            pltpu.VMEM((2 * chunks, depth, width), jnp.float32),
            pltpu.VMEM((cg, rows, depth), jnp.bfloat16),
            pltpu.VMEM((2, depth, span), jnp.bfloat16),
            pltpu.VMEM((2, 2, rows, span), jnp.bfloat16),
            pltpu.SemaphoreType.DMA((2, 2, spots)),
        ],
        compiler_params=pltpu.CompilerParams(vmem_limit_bytes=VMEM_BYTES),
    )(*operands)


def turn_plane(value, i):
    planes, rows = lax.axis_size("chan"), lax.axis_size("row")
    steps = plane_steps(planes)
    pairs = []
    for c in range(planes):
        for r in range(rows):
            pairs.append((c * rows + r, (c ^ steps[r % 2][i]) * rows + r - r % 2 + c % 2))
    return lax.ppermute(value, ("chan", "row"), pairs)


def swapped(value):
    peers = lax.axis_size(FRAME_AXES)
    return lax.ppermute(value, FRAME_AXES, [(i, i ^ 1) for i in range(peers)])


def local(samples, channel_index, gain_real, gain_imag, flags):
    planes = lax.axis_size("chan")
    chips = lax.axis_size(FRAME_AXES) // 2
    inputs_total = samples.shape[2] * planes
    keep, give = front(samples, channel_index, gain_real, gain_imag, flags, planes)
    here, following, after = pair_sum(keep, swapped(give))
    after = rotated(after, FRAME_AXES, 4)
    following = rotated(following, FRAME_AXES, 2)
    pieces = combine(here, following, after, planes // 2)
    pieces = jnp.stack([turn_plane(piece, j) for j, piece in enumerate(pieces)])
    peers = 2 * chips
    mine = jnp.stack([pieces] + [lax.ppermute(pieces, FRAME_AXES, [(i, i ^ (2 * s)) for i in range(peers)]) for s in range(1, chips)])
    other = swapped(mine)
    rows, cols = inputs_total // lax.axis_size("row"), inputs_total // lax.axis_size("tm")
    width = samples.shape[2]
    if rows != width or cols != 2 * width:
        return correlate([mine, other], rows, cols, None)
    near = correlate([mine], rows, cols, 0)
    return correlate([mine, other, near], rows, cols, 1)


def solution(mesh):
    in_specs = (P(("tm", "row"), None, "chan"), P(), P(None, "chan"), P(None, "chan"), P("chan"))
    out_specs = P(None, "chan", "row", "tm")
    return jax.shard_map(local, mesh=mesh, in_specs=in_specs, out_specs=out_specs, check_vma=False)
```
